128 devices in a mesh: row: 8 (over x_lo, z), col: 16 (over x_hi, y, core).
Axes of the slice: x: 4 (x_hi: 2, x_lo: 2; x = x_hi * 2 + x_lo), y: 4, z: 4, core: 2. Of those that a mesh axis runs over, the one named last changes fastest.
Arguments:
- level_set: float32 [384, 384, 384], P('col', 'row'), may hold values from -7 to 7
- image: float32 [384, 384, 384], P('col', 'row'), may hold values from -6 to 6
Outputs:
- updated_level: float32 [384, 384, 384], P('col', 'row')
The draws below stay inside these ranges and needn't reach their ends.
All inputs are finite; a program needn't handle non-finite values.
Results may differ from the reference program's by a relative error of at most 0.00021.
Values sent between devices are 32-bit elements; how exact they have to be, the bound alone decides.
A program may use at most 128 MiB of HBM per device.

```python
import jax
import jax.numpy as jnp

N = 384
RADIUS = 6


def pattern_field(key):
    base = jax.random.fold_in(key, 7)
    wave_numbers = jax.random.randint(jax.random.fold_in(base, 1), (3, 3), 1, 4).astype(jnp.float32)
    phases = jax.random.uniform(jax.random.fold_in(base, 2), (3,), jnp.float32, -3.14159, 3.14159)
    coord_z = jnp.arange(N, dtype=jnp.float32).reshape(N, 1, 1)
    coord_y = jnp.arange(N, dtype=jnp.float32).reshape(1, N, 1)
    coord_x = jnp.arange(N, dtype=jnp.float32).reshape(1, 1, N)
    summed = jnp.zeros((N, N, N), jnp.float32)
    for which in range(3):
        angle = 2.0 * 3.14159265 * (wave_numbers[which, 0] * coord_z + wave_numbers[which, 1] * coord_y + wave_numbers[which, 2] * coord_x) / N + phases[which]
        summed = summed + jnp.cos(angle)
    return summed / 1.2247


def noise_field(key, label, limit):
    noise_key = jax.random.fold_in(key, label)
    return jax.random.truncated_normal(noise_key, -limit, limit, (N, N, N), jnp.float32)


def alternation(key, label):
    base = jax.random.fold_in(key, label)
    strength = 0.35
    sign_draw = jnp.where(jax.random.bernoulli(base, 0.5, (3,)), 1.0, -1.0).astype(jnp.float32)
    parity = (jnp.arange(N, dtype=jnp.int32) % 2).astype(jnp.float32)
    flip_sign = 1.0 - 2.0 * parity
    return strength * (sign_draw[0] * flip_sign.reshape(N, 1, 1) + sign_draw[1] * flip_sign.reshape(1, N, 1) + sign_draw[2] * flip_sign.reshape(1, 1, N))


def draw_level_set(key, part):
    return 0.8 * pattern_field(key) + noise_field(key, 11, 3.9) + alternation(key, 17)


def draw_image(key, part):
    return pattern_field(key) + 0.7 * noise_field(key, 13, 3.5) + alternation(key, 19)


def setup_inputs(seed: int = 0) -> dict:
    seeds = jax.random.split(jax.random.key(seed), 3)
    return {
        "level_set": draw_level_set(jax.random.fold_in(seeds[2], 71), 0),
        "image": draw_image(jax.random.fold_in(seeds[2], 71), 0),
    }


sigma_cells = 8.0
dt_step = 0.5
nu_diff = 0.1
eps_fit = 0.05


def kernel_row(length):
    indices = jnp.arange(length, dtype=jnp.int32)
    distance = jnp.minimum(indices, length - indices)
    spacing = distance.astype(jnp.float32)
    weights = jnp.where(distance <= RADIUS, jnp.exp(-spacing * spacing / (2.0 * sigma_cells * sigma_cells)), 0.0)
    return weights / jnp.sum(weights)


def smooth(volume, kernel_spec):
    for which_axis in range(3):
        spectrum = jnp.fft.rfft(volume, axis=which_axis)
        shape_list = [1, 1, 1]
        shape_list[which_axis] = kernel_spec.shape[0]
        volume = jnp.fft.irfft(spectrum * kernel_spec.reshape(shape_list), n=N, axis=which_axis)
        volume = volume.astype(jnp.float32)
    return volume


def reference(level_set, image):
    heaviside = 0.5 + jnp.arctan(level_set) / jnp.pi
    kernel_spec = jnp.fft.rfft(kernel_row(N))
    first = smooth(heaviside * image, kernel_spec)
    second = smooth(heaviside, kernel_spec)
    third = smooth(image, kernel_spec)
    fourth = smooth(image * image, kernel_spec)
    inside_mean = first / (second + eps_fit)
    outside_mean = (third - first) / (1.0 - second + eps_fit)
    spread = fourth - third * third + eps_fit
    slope_term = 2.0 * (inside_mean - outside_mean) / spread
    offset = (outside_mean * outside_mean - inside_mean * inside_mean) / spread
    forcing = image * slope_term + offset
    laplace = (jnp.roll(level_set, 1, 0) + jnp.roll(level_set, -1, 0)
               + jnp.roll(level_set, 1, 1) + jnp.roll(level_set, -1, 1)
               + jnp.roll(level_set, 1, 2) + jnp.roll(level_set, -1, 2) - 6.0 * level_set)
    dirac_weight = 1.0 / (jnp.pi * (1.0 + level_set * level_set))
    return level_set + dt_step * (nu_diff * laplace + dirac_weight * forcing)
```

```python
import functools

import jax
import jax.numpy as jnp
import ml_dtypes
import numpy as np
from jax import lax
from jax.experimental import pallas as pl
from jax.experimental.pallas import tpu as pltpu
from jax.sharding import PartitionSpec as P

R = 6
N = 384
ZL, YL = 24, 48
ZE, YE = ZL + 2 * R, YL + 16
EPS = 0.05
SIGMA = 8.0
DT, NU = 0.5, 0.1
G = 4
F32, BF16 = jnp.float32, jnp.bfloat16
MESH = pl.DeviceIdType.MESH

ATAN = (
    0.3183096647262573, -0.10609224438667297, 0.06349188834428787, -0.044272541999816895,
    0.03069206140935421, -0.0177974384278059, 0.006959190126508474, -0.0012906072661280632,
)


def taps():
    offsets = np.arange(-R, R + 1, dtype=np.float64)
    weights = np.exp(-offsets * offsets / (2.0 * SIGMA * SIGMA))
    return weights / weights.sum()


def split(table):
    high = table.astype(np.float32).astype(ml_dtypes.bfloat16)
    low = (table - high.astype(np.float64)).astype(np.float32).astype(ml_dtypes.bfloat16)
    return high, low


def tables():
    weights = taps()

    def tap(distance):
        return weights[R + distance] if abs(distance) <= R else 0.0

    centre = weights[R]
    source = list(range(YL)) + list(range(-8, 0)) + list(range(YL, YL + 8))

    def block(outs, cols):
        one = np.array([[tap(source[c] - o) * centre for c in cols] for o in outs])
        return np.kron(np.eye(G), one)

    inner = block(range(8, 40), range(YL))
    edge = block(list(range(8)) + list(range(40, 48)), range(YE))
    i = np.arange(N)
    d = np.abs(i[:, None] - i[None, :])
    d = np.minimum(d, N - d)
    along_x = np.where(d <= R, weights[np.minimum(R + d, 2 * R)], 0.0)
    return split(inner) + split(edge) + split(along_x)


def heaviside(level):
    size = jnp.abs(level)
    big = size > 1.0
    t = jnp.where(big, 1.0 / jnp.maximum(size, 1.0), size)
    u = t * t
    q = jnp.full_like(u, ATAN[-1])
    for coeff in ATAN[-2::-1]:
        q = q * u + coeff
    q = q * t
    q = jnp.where(big, 0.5 - q, q)
    return 0.5 + jnp.where(level < 0.0, -q, q)


def kernel(level_hbm, image_hbm, yi_h, yi_l, ye_h, ye_l, x_h, x_l, out_ref,
           lev, img, hv, hi, ii, g_h, g_l, xs_h, xs_l, sm,
           t_yih, t_yil, t_yeh, t_yel, t_xh, t_xl,
           local_sem, send_sem, recv_sem):
    row, col = lax.axis_index("row"), lax.axis_index("col")
    n_row, n_col = lax.axis_size("row"), lax.axis_size("col")
    r_up, r_dn = lax.rem(row + 1, n_row), lax.rem(row + n_row - 1, n_row)
    c_up, c_dn = lax.rem(col + 1, n_col), lax.rem(col + n_col - 1, n_col)

    barrier = pltpu.get_barrier_semaphore()
    around = [{"row": r, "col": c} for r in (r_dn, row, r_up) for c in (c_dn, col, c_up)]
    del around[4]
    for device in around:
        pl.semaphore_signal(barrier, inc=1, device_id=device, device_id_type=MESH)

    own = []
    for i, (src, dst) in enumerate((
        (level_hbm, lev.at[R:R + ZL, 0:YL]), (image_hbm, img.at[R:R + ZL, 0:YL]),
        (yi_h, t_yih), (yi_l, t_yil), (ye_h, t_yeh), (ye_l, t_yel), (x_h, t_xh), (x_l, t_xl),
    )):
        copy = pltpu.make_async_copy(src, dst, local_sem.at[i])
        copy.start()
        own.append(copy)

    pl.semaphore_wait(barrier, 8)

    z_src = {1: pl.ds(ZL - R, R), 0: pl.ds(0, ZL), -1: pl.ds(0, R)}
    z_dst = {1: pl.ds(0, R), 0: pl.ds(R, ZL), -1: pl.ds(R + ZL, R)}
    y_src = {1: pl.ds(YL - 8, 8), 0: pl.ds(0, YL), -1: pl.ds(0, 8)}
    y_dst = {1: pl.ds(YL, 8), 0: pl.ds(0, YL), -1: pl.ds(YL + 8, 8)}
    rows_of, cols_of = {1: r_up, 0: row, -1: r_dn}, {1: c_up, 0: col, -1: c_dn}
    remote = {}
    order = [(0, 1), (0, -1), (1, 0), (-1, 0), (1, 1), (1, -1), (-1, 1), (-1, -1)]
    for k, (dr, dc) in enumerate(order):
        for a, (src, dst) in enumerate(((level_hbm, lev), (image_hbm, img))):
            copy = pltpu.make_async_remote_copy(
                src_ref=src.at[z_src[dc], y_src[dr]],
                dst_ref=dst.at[z_dst[dc], y_dst[dr]],
                send_sem=send_sem.at[k, a],
                recv_sem=recv_sem.at[k, a],
                device_id={"row": rows_of[dr], "col": cols_of[dc]},
                device_id_type=MESH,
            )
            copy.start()
            remote[k, a] = copy

    def fields(first, count, start, size, step):
        @pl.loop(first, first + count)
        def _(p):
            for s in range(start, start + size, step):
                rows = slice(s, s + step)
                h = heaviside(lev[p, rows, :])
                im = img[p, rows, :]
                hv[p, rows, :] = h
                hi[p, rows, :] = h * im
                ii[p, rows, :] = im * im

    weights = taps()
    ratio = [float(np.float32(weights[R + d] / weights[R])) for d in range(R + 1)]

    def smooth_z(g, chunks):
        for k, ref in enumerate((hi, hv, img, ii)):
            for rc in chunks:
                rows = slice(rc * 16, rc * 16 + 16)
                for lt in range(3):
                    lanes = slice(lt * 128, lt * 128 + 128)
                    f = [ref[g * G + j, rows, lanes] for j in range(G + 2 * R)]
                    for o in range(G):
                        total = f[o + R]
                        for d in range(1, R + 1):
                            total = total + ratio[d] * (f[o + R - d] + f[o + R + d])
                        high = total.astype(BF16)
                        g_h[k, g * G + o, rows, lanes] = high
                        g_l[k, g * G + o, rows, lanes] = (total - high.astype(F32)).astype(BF16)

    def dot(a, b):
        return jnp.dot(a, b, preferred_element_type=F32)

    def finish(g, t_h, t_l, depth, rows_out):
        m = G * rows_out
        planes = pl.ds(g * G, G)
        for k in range(4):
            high = g_h[k, planes, 0:depth, :].reshape(G * depth, N)
            low = g_l[k, planes, 0:depth, :].reshape(G * depth, N)
            y = dot(t_h[...], high) + dot(t_l[...], high) + dot(t_h[...], low)
            yh = y.astype(BF16)
            xs_h[k * m:(k + 1) * m, :] = yh
            xs_l[k * m:(k + 1) * m, :] = (y - yh.astype(F32)).astype(BF16)
        a = xs_h[0:4 * m, :]
        sm[0:4 * m, :] = dot(a, t_xh[...]) + dot(a, t_xl[...]) + dot(xs_l[0:4 * m, :], t_xh[...])

    def pointwise(p, rows, s_rows, up, down):
        base, stride = s_rows
        s1, s2, s3, s4 = (sm[pl.ds(base + k * stride, rows.stop - rows.start), :] for k in range(4))
        level = lev[p + R, rows, :]
        im = img[p + R, rows, :]
        inner = s2 + EPS
        outer = 1.0 - s2 + EPS
        rest = s3 - s1
        both = inner * outer
        x1, x2 = s1 * outer, rest * inner
        spread = s4 - s3 * s3 + EPS
        force = (x1 - x2) * (2.0 * im * both - (x1 + x2)) / (both * both * spread * (np.pi * (1.0 + level * level)))
        lap = (lev[p + R + 1, rows, :] + lev[p + R - 1, rows, :] + up + down
               + pltpu.roll(level, 1, 1) + pltpu.roll(level, N - 1, 1) - 6.0 * level)
        out_ref[p, rows, :] = level + DT * (NU * lap + force)

    def inner_group(g):
        smooth_z(g, range(3))
        finish(g, t_yih, t_yil, YL, 32)

        @pl.loop(0, G)
        def _(o):
            p = g * G + o
            for s in range(8, 40, 8):
                pointwise(p, slice(s, s + 8), (o * 32 + s - 8, G * 32),
                          lev[p + R, s + 1:s + 9, :], lev[p + R, s - 1:s + 7, :])

    def edge_group(g):
        smooth_z(g, range(3, 4))
        finish(g, t_yeh, t_yel, YE, 16)

        @pl.loop(0, G)
        def _(o):
            p = g * G + o
            sub = lax.broadcasted_iota(jnp.int32, (8, N), 0)
            level = lev[p + R, 0:8, :]
            before = lev[p + R, YL:YL + 8, :]
            down = jnp.where(sub == 0, pltpu.roll(before, 1, 0), pltpu.roll(level, 1, 0))
            pointwise(p, slice(0, 8), (o * 16, G * 16), lev[p + R, 1:9, :], down)
            level = lev[p + R, 40:48, :]
            after = lev[p + R, YL + 8:YL + 16, :]
            up = jnp.where(sub == 7, pltpu.roll(after, 7, 0), pltpu.roll(level, 7, 0))
            pointwise(p, slice(40, 48), (o * 16 + 8, G * 16), up, lev[p + R, 39:47, :])

    for copy in own:
        copy.wait()
    fields(R, ZL, 0, YL, 16)
    pl.loop(2, 4)(inner_group)

    for k in (0, 1):
        for a in (0, 1):
            remote[k, a].wait_recv()
    fields(0, R, 0, YL, 16)
    fields(R + ZL, R, 0, YL, 16)
    pl.loop(0, 2)(inner_group)
    pl.loop(4, 6)(inner_group)

    for k in range(2, 8):
        for a in (0, 1):
            remote[k, a].wait_recv()
    fields(0, ZE, YL, 16, 16)
    pl.loop(0, 6)(edge_group)

    for k in range(8):
        for a in (0, 1):
            remote[k, a].wait_send()


def step(level_set, image):
    consts = [jnp.asarray(t) for t in tables()]
    ext = pltpu.VMEM((ZE, YE, N), F32)
    half = pltpu.VMEM((4, ZL, YE, N), BF16)
    rows = 4 * G * 32
    return pl.pallas_call(
        kernel,
        out_shape=jax.ShapeDtypeStruct((ZL, YL, N), F32),
        in_specs=[pl.BlockSpec(memory_space=pl.ANY)] * 8,
        out_specs=pl.BlockSpec(memory_space=pltpu.VMEM),
        scratch_shapes=[ext] * 5 + [half, half, pltpu.VMEM((rows, N), BF16), pltpu.VMEM((rows, N), BF16),
                                    pltpu.VMEM((rows, N), F32)]
        + [pltpu.VMEM(c.shape, BF16) for c in consts]
        + [pltpu.SemaphoreType.DMA((8,)), pltpu.SemaphoreType.DMA((8, 2)), pltpu.SemaphoreType.DMA((8, 2))],
        compiler_params=pltpu.CompilerParams(
            collective_id=0, has_side_effects=True, vmem_limit_bytes=48 * 1024 * 1024),
    )(level_set, image, *consts)


def solution(mesh):
    return jax.shard_map(
        step,
        mesh=mesh,
        in_specs=(P("col", "row", None), P("col", "row", None)),
        out_specs=P("col", "row", None),
        check_vma=False,
    )
```

```python
import functools

import jax
import jax.numpy as jnp
import ml_dtypes
import numpy as np
from jax import lax
from jax.experimental import pallas as pl
from jax.experimental.pallas import tpu as pltpu
from jax.sharding import PartitionSpec as P

R = 6
N = 384
ZL, YL = 24, 48
ZE, YE = ZL + 2 * R, YL + 16
EPS = 0.05
SIGMA = 8.0
DT, NU = 0.5, 0.1
G = 4
F32, BF16 = jnp.float32, jnp.bfloat16
MESH = pl.DeviceIdType.MESH

ATAN = (
    0.3183096647262573, -0.10609224438667297, 0.06349188834428787, -0.044272541999816895,
    0.03069206140935421, -0.0177974384278059, 0.006959190126508474, -0.0012906072661280632,
)


def taps():
    offsets = np.arange(-R, R + 1, dtype=np.float64)
    weights = np.exp(-offsets * offsets / (2.0 * SIGMA * SIGMA))
    return weights / weights.sum()


def split(table):
    high = table.astype(np.float32).astype(ml_dtypes.bfloat16)
    low = (table - high.astype(np.float64)).astype(np.float32).astype(ml_dtypes.bfloat16)
    return high, low


def tables():
    weights = taps()

    def tap(distance):
        return weights[R + distance] if abs(distance) <= R else 0.0

    centre = weights[R]
    source = list(range(YL)) + list(range(-8, 0)) + list(range(YL, YL + 8))

    def block(outs, cols):
        one = np.array([[tap(source[c] - o) * centre for c in cols] for o in outs])
        return np.kron(np.eye(G), one)

    inner = block(range(8, 40), range(YL))
    edge = block(list(range(8)) + list(range(40, 48)), range(YE))
    i = np.arange(N)
    d = np.abs(i[:, None] - i[None, :])
    d = np.minimum(d, N - d)
    along_x = np.where(d <= R, weights[np.minimum(R + d, 2 * R)], 0.0)
    return split(inner) + split(edge) + split(along_x)


def heaviside(level):
    size = jnp.abs(level)
    big = size > 1.0
    t = jnp.where(big, 1.0 / jnp.maximum(size, 1.0), size)
    u = t * t
    q = jnp.full_like(u, ATAN[-1])
    for coeff in ATAN[-2::-1]:
        q = q * u + coeff
    q = q * t
    q = jnp.where(big, 0.5 - q, q)
    return 0.5 + jnp.where(level < 0.0, -q, q)


def kernel(level_hbm, image_hbm, yi_h, yi_l, ye_h, ye_l, x_h, x_l, out_ref,
           lev, img, hv, hi, ii, g_h, g_l, xs_h, xs_l, sm,
           t_yih, t_yil, t_yeh, t_yel, t_xh, t_xl,
           local_sem, send_sem, recv_sem):
    row, col = lax.axis_index("row"), lax.axis_index("col")
    n_row, n_col = lax.axis_size("row"), lax.axis_size("col")
    r_up, r_dn = lax.rem(row + 1, n_row), lax.rem(row + n_row - 1, n_row)
    c_up, c_dn = lax.rem(col + 1, n_col), lax.rem(col + n_col - 1, n_col)

    barrier = pltpu.get_barrier_semaphore()
    for device in ({"row": row, "col": c_up}, {"row": row, "col": c_dn}, {"row": r_up, "col": col}, {"row": r_dn, "col": col}):
        pl.semaphore_signal(barrier, inc=1, device_id=device, device_id_type=MESH)

    own = []
    for i, (src, dst) in enumerate((
        (level_hbm, lev.at[R:R + ZL, 0:YL]), (image_hbm, img.at[R:R + ZL, 0:YL]),
        (yi_h, t_yih), (yi_l, t_yil), (ye_h, t_yeh), (ye_l, t_yel), (x_h, t_xh), (x_l, t_xl),
    )):
        copy = pltpu.make_async_copy(src, dst, local_sem.at[i])
        copy.start()
        own.append(copy)

    pl.semaphore_wait(barrier, 4)

    sent = {}

    def send(name, axis, target, src_level, src_image, dst):
        for a, (src, to) in enumerate(((src_level, lev), (src_image, img))):
            i = len(sent)
            copy = pltpu.make_async_remote_copy(
                src_ref=src, dst_ref=to.at[dst], send_sem=send_sem.at[i], recv_sem=recv_sem.at[i],
                device_id={axis: target}, device_id_type=MESH,
            )
            copy.start()
            sent[name, a] = copy

    def arrived(*parts):
        for name in parts:
            for a in (0, 1):
                sent[name, a].wait_recv()

    low, high, middle = pl.ds(0, R), pl.ds(ZL - R, R), pl.ds(R, ZL - 2 * R)
    first_rows, last_rows = pl.ds(0, 8), pl.ds(YL - 8, 8)

    def send_rows(name, planes, first):
        for way, target, rows, to in ((0, r_up, last_rows, YL), (1, r_dn, first_rows, YL + 8)):
            send((name, way), "row", target, level_hbm.at[planes, rows], image_hbm.at[planes, rows],
                 (pl.ds(R + first, planes.size), pl.ds(to, 8)))

    send_rows("low", low, 0)
    send_rows("high", high, ZL - R)
    own_rows = pl.ds(0, YL)
    send("above", "col", c_up, level_hbm.at[high], image_hbm.at[high], (pl.ds(0, R), own_rows))
    send("below", "col", c_dn, level_hbm.at[low], image_hbm.at[low], (pl.ds(R + ZL, R), own_rows))
    send_rows("middle", middle, R)

    def fields(first, count, start, size, step):
        @pl.loop(first, first + count)
        def _(p):
            for s in range(start, start + size, step):
                rows = slice(s, s + step)
                h = heaviside(lev[p, rows, :])
                im = img[p, rows, :]
                hv[p, rows, :] = h
                hi[p, rows, :] = h * im
                ii[p, rows, :] = im * im

    weights = taps()
    ratio = [float(np.float32(weights[R + d] / weights[R])) for d in range(R + 1)]

    def smooth_z(g, chunks):
        for k, ref in enumerate((hi, hv, img, ii)):
            for rc in chunks:
                rows = slice(rc * 16, rc * 16 + 16)
                for lt in range(3):
                    lanes = slice(lt * 128, lt * 128 + 128)
                    f = [ref[g * G + j, rows, lanes] for j in range(G + 2 * R)]
                    for o in range(G):
                        total = f[o + R]
                        for d in range(1, R + 1):
                            total = total + ratio[d] * (f[o + R - d] + f[o + R + d])
                        high = total.astype(BF16)
                        g_h[k, g * G + o, rows, lanes] = high
                        g_l[k, g * G + o, rows, lanes] = (total - high.astype(F32)).astype(BF16)

    def dot(a, b):
        return jnp.dot(a, b, preferred_element_type=F32)

    def finish(g, t_h, t_l, depth, rows_out):
        m = G * rows_out
        planes = pl.ds(g * G, G)
        for k in range(4):
            high = g_h[k, planes, 0:depth, :].reshape(G * depth, N)
            low = g_l[k, planes, 0:depth, :].reshape(G * depth, N)
            y = dot(t_h[...], high) + dot(t_l[...], high) + dot(t_h[...], low)
            yh = y.astype(BF16)
            xs_h[k * m:(k + 1) * m, :] = yh
            xs_l[k * m:(k + 1) * m, :] = (y - yh.astype(F32)).astype(BF16)
        a = xs_h[0:4 * m, :]
        sm[0:4 * m, :] = dot(a, t_xh[...]) + dot(a, t_xl[...]) + dot(xs_l[0:4 * m, :], t_xh[...])

    def pointwise(p, rows, s_rows, up, down):
        base, stride = s_rows
        s1, s2, s3, s4 = (sm[pl.ds(base + k * stride, rows.stop - rows.start), :] for k in range(4))
        level = lev[p + R, rows, :]
        im = img[p + R, rows, :]
        inner = s2 + EPS
        outer = 1.0 - s2 + EPS
        rest = s3 - s1
        both = inner * outer
        x1, x2 = s1 * outer, rest * inner
        spread = s4 - s3 * s3 + EPS
        force = (x1 - x2) * (2.0 * im * both - (x1 + x2)) / (both * both * spread * (np.pi * (1.0 + level * level)))
        lap = (lev[p + R + 1, rows, :] + lev[p + R - 1, rows, :] + up + down
               + pltpu.roll(level, 1, 1) + pltpu.roll(level, N - 1, 1) - 6.0 * level)
        out_ref[p, rows, :] = level + DT * (NU * lap + force)

    def inner_group(g):
        smooth_z(g, range(3))
        finish(g, t_yih, t_yil, YL, 32)

        @pl.loop(0, G)
        def _(o):
            p = g * G + o
            for s in range(8, 40, 8):
                pointwise(p, slice(s, s + 8), (o * 32 + s - 8, G * 32),
                          lev[p + R, s + 1:s + 9, :], lev[p + R, s - 1:s + 7, :])

    def edge_group(g):
        smooth_z(g, range(3, 4))
        finish(g, t_yeh, t_yel, YE, 16)

        @pl.loop(0, G)
        def _(o):
            p = g * G + o
            sub = lax.broadcasted_iota(jnp.int32, (8, N), 0)
            level = lev[p + R, 0:8, :]
            before = lev[p + R, YL:YL + 8, :]
            down = jnp.where(sub == 0, pltpu.roll(before, 1, 0), pltpu.roll(level, 1, 0))
            pointwise(p, slice(0, 8), (o * 16, G * 16), lev[p + R, 1:9, :], down)
            level = lev[p + R, 40:48, :]
            after = lev[p + R, YL + 8:YL + 16, :]
            up = jnp.where(sub == 7, pltpu.roll(after, 7, 0), pltpu.roll(level, 7, 0))
            pointwise(p, slice(40, 48), (o * 16 + 8, G * 16), up, lev[p + R, 39:47, :])

    for copy in own:
        copy.wait()
    fields(R, ZL, 0, YL, 16)
    pl.loop(2, 4)(inner_group)

    arrived(("low", 0), ("low", 1), ("high", 0), ("high", 1))
    halo_rows = pl.ds(YL, 16)
    top, bottom = pl.ds(ZL, R), pl.ds(R, R)
    send("corner above", "col", c_up, lev.at[top, halo_rows], img.at[top, halo_rows], (pl.ds(0, R), halo_rows))
    send("corner below", "col", c_dn, lev.at[bottom, halo_rows], img.at[bottom, halo_rows],
         (pl.ds(R + ZL, R), halo_rows))

    arrived("above", "below")
    fields(0, R, 0, YL, 16)
    fields(R + ZL, R, 0, YL, 16)
    pl.loop(0, 2)(inner_group)
    pl.loop(4, 6)(inner_group)

    arrived(("middle", 0), ("middle", 1), "corner above", "corner below")
    fields(0, ZE, YL, 16, 16)
    pl.loop(0, 6)(edge_group)

    for copy in sent.values():
        copy.wait_send()


def step(level_set, image):
    consts = [jnp.asarray(t) for t in tables()]
    ext = pltpu.VMEM((ZE, YE, N), F32)
    half = pltpu.VMEM((4, ZL, YE, N), BF16)
    rows = 4 * G * 32
    return pl.pallas_call(
        kernel,
        out_shape=jax.ShapeDtypeStruct((ZL, YL, N), F32),
        in_specs=[pl.BlockSpec(memory_space=pltpu.HBM)] * 8,
        out_specs=pl.BlockSpec(memory_space=pltpu.VMEM),
        scratch_shapes=[ext] * 5 + [half, half, pltpu.VMEM((rows, N), BF16), pltpu.VMEM((rows, N), BF16),
                                    pltpu.VMEM((rows, N), F32)]
        + [pltpu.VMEM(c.shape, BF16) for c in consts]
        + [pltpu.SemaphoreType.DMA((8,)), pltpu.SemaphoreType.DMA((20,)), pltpu.SemaphoreType.DMA((20,))],
        compiler_params=pltpu.CompilerParams(
            collective_id=0, has_side_effects=True, vmem_limit_bytes=48 * 1024 * 1024),
    )(*[pltpu.with_memory_space_constraint(v, pltpu.HBM) for v in (level_set, image, *consts)])


def solution(mesh):
    return jax.shard_map(
        step,
        mesh=mesh,
        in_specs=(P("col", "row", None), P("col", "row", None)),
        out_specs=P("col", "row", None),
        check_vma=False,
    )
```

```python
import functools

import jax
import jax.numpy as jnp
import ml_dtypes
import numpy as np
from jax import lax
from jax.experimental import pallas as pl
from jax.experimental.pallas import tpu as pltpu
from jax.sharding import PartitionSpec as P

R = 6
N = 384
ZL, YL = 24, 48
ZE, YE = ZL + 2 * R, YL + 16
EPS = 0.05
SIGMA = 8.0
DT, NU = 0.5, 0.1
G = 4
F32, BF16 = jnp.float32, jnp.bfloat16
MESH = pl.DeviceIdType.MESH

ATAN = (
    0.3183096647262573, -0.10609224438667297, 0.06349188834428787, -0.044272541999816895,
    0.03069206140935421, -0.0177974384278059, 0.006959190126508474, -0.0012906072661280632,
)


def taps():
    offsets = np.arange(-R, R + 1, dtype=np.float64)
    weights = np.exp(-offsets * offsets / (2.0 * SIGMA * SIGMA))
    return weights / weights.sum()


def split(table):
    high = table.astype(np.float32).astype(ml_dtypes.bfloat16)
    low = (table - high.astype(np.float64)).astype(np.float32).astype(ml_dtypes.bfloat16)
    return high, low


def tables():
    weights = taps()

    def tap(distance):
        return weights[R + distance] if abs(distance) <= R else 0.0

    centre = weights[R]
    source = list(range(YL)) + list(range(-8, 0)) + list(range(YL, YL + 8))

    def block(outs, cols):
        one = np.array([[tap(source[c] - o) * centre for c in cols] for o in outs])
        return np.kron(np.eye(G), one)

    inner = block(range(8, 40), range(YL))
    edge = block(list(range(8)) + list(range(40, 48)), range(YE))
    i = np.arange(N)
    d = np.abs(i[:, None] - i[None, :])
    d = np.minimum(d, N - d)
    along_x = np.where(d <= R, weights[np.minimum(R + d, 2 * R)], 0.0)
    return tuple(np.concatenate(split(t)) for t in (inner, edge)) + split(along_x)


def heaviside(level):
    size = jnp.abs(level)
    big = size > 1.0
    t = jnp.where(big, 1.0 / jnp.maximum(size, 1.0), size)
    u = t * t
    q = jnp.full_like(u, ATAN[-1])
    for coeff in ATAN[-2::-1]:
        q = q * u + coeff
    q = q * t
    q = jnp.where(big, 0.5 - q, q)
    return 0.5 + jnp.where(level < 0.0, -q, q)


def kernel(level_hbm, image_hbm, y_in, y_ed, x_h, x_l, out_ref,
           lev, img, hv, hi, ii, g_h, g_l, xs_h, xs_l, sm,
           t_yi, t_ye, t_xh, t_xl,
           local_sem, send_sem, recv_sem):
    row, col = lax.axis_index("row"), lax.axis_index("col")
    n_row, n_col = lax.axis_size("row"), lax.axis_size("col")
    r_up, r_dn = lax.rem(row + 1, n_row), lax.rem(row + n_row - 1, n_row)
    c_up, c_dn = lax.rem(col + 1, n_col), lax.rem(col + n_col - 1, n_col)

    barrier = pltpu.get_barrier_semaphore()
    for device in ({"row": row, "col": c_up}, {"row": row, "col": c_dn}, {"row": r_up, "col": col}, {"row": r_dn, "col": col}):
        pl.semaphore_signal(barrier, inc=1, device_id=device, device_id_type=MESH)

    own = []
    for i, (src, dst) in enumerate((
        (level_hbm, lev.at[R:R + ZL, 0:YL]), (image_hbm, img.at[R:R + ZL, 0:YL]),
        (y_in, t_yi), (y_ed, t_ye), (x_h, t_xh), (x_l, t_xl),
    )):
        copy = pltpu.make_async_copy(src, dst, local_sem.at[i])
        copy.start()
        own.append(copy)

    pl.semaphore_wait(barrier, 4)

    sent = {}

    def send(name, axis, target, src_level, src_image, dst, now=True):
        for a, (src, to) in enumerate(((src_level, lev), (src_image, img))):
            i = len(sent)
            copy = pltpu.make_async_remote_copy(
                src_ref=src, dst_ref=to.at[dst], send_sem=send_sem.at[i], recv_sem=recv_sem.at[i],
                device_id={axis: target}, device_id_type=MESH,
            )
            if now:
                copy.start()
            sent[name, a] = copy

    def arrived(*parts):
        for name in parts:
            for a in (0, 1):
                sent[name, a].wait_recv()

    low, high, middle = pl.ds(0, R), pl.ds(ZL - R, R), pl.ds(R, ZL - 2 * R)
    first_rows, last_rows = pl.ds(0, 8), pl.ds(YL - 8, 8)

    def send_rows(name, planes, first):
        for way, target, rows, to in ((0, r_up, last_rows, YL), (1, r_dn, first_rows, YL + 8)):
            send((name, way), "row", target, level_hbm.at[planes, rows], image_hbm.at[planes, rows],
                 (pl.ds(R + first, planes.size), pl.ds(to, 8)))

    send_rows("low", low, 0)
    send_rows("high", high, ZL - R)
    send_rows("middle", middle, R)
    own_rows = pl.ds(0, YL)
    send("above", "col", c_up, level_hbm.at[high], image_hbm.at[high], (pl.ds(0, R), own_rows))
    send("below", "col", c_dn, level_hbm.at[low], image_hbm.at[low], (pl.ds(R + ZL, R), own_rows))
    halo_rows = pl.ds(YL, 16)
    top, bottom = pl.ds(ZL, R), pl.ds(R, R)
    send("corner above", "col", c_up, lev.at[top, halo_rows], img.at[top, halo_rows], (pl.ds(0, R), halo_rows), False)
    send("corner below", "col", c_dn, lev.at[bottom, halo_rows], img.at[bottom, halo_rows],
         (pl.ds(R + ZL, R), halo_rows), False)

    def fields(first, count, start, size, step):
        @pl.loop(first, first + count)
        def _(p):
            for s in range(start, start + size, step):
                rows = slice(s, s + step)
                h = heaviside(lev[p, rows, :])
                im = img[p, rows, :]
                hv[p, rows, :] = h
                hi[p, rows, :] = h * im
                ii[p, rows, :] = im * im

    weights = taps()
    ratio = [float(np.float32(weights[R + d] / weights[R])) for d in range(R + 1)]

    def smooth_z(g, chunk):
        rows = slice(chunk * 16, chunk * 16 + 16)
        for k, ref in enumerate((hi, hv, img, ii)):
            for lt in range(3):
                lanes = slice(lt * 128, lt * 128 + 128)
                f = [ref[g * G + j, rows, lanes] for j in range(G + 2 * R)]
                for o in range(G):
                    total = f[o + R]
                    for d in range(1, R + 1):
                        total = total + ratio[d] * (f[o + R - d] + f[o + R + d])
                    high = total.astype(BF16)
                    g_h[k, g * G + o, rows, lanes] = high
                    g_l[k, g * G + o, rows, lanes] = (total - high.astype(F32)).astype(BF16)

    def dot(a, b):
        return jnp.dot(a, b, preferred_element_type=F32)

    def smooth_y(g, table, depth, base):
        planes = pl.ds(g * G, G)
        m = table.shape[0] // 2
        for k in range(4):
            high = g_h[k, planes, 0:depth, :].reshape(G * depth, N)
            low = g_l[k, planes, 0:depth, :].reshape(G * depth, N)
            y = dot(table[...], high)
            y = y[0:m] + y[m:2 * m] + dot(table[0:m, :], low)
            yh = y.astype(BF16)
            xs_h[k * 128 + base:k * 128 + base + m, :] = yh
            xs_l[k * 128 + base:k * 128 + base + m, :] = (y - yh.astype(F32)).astype(BF16)

    def smooth_x():
        a = xs_h[...]
        sm[...] = dot(a, t_xh[...]) + dot(a, t_xl[...]) + dot(xs_l[...], t_xh[...])

    def pointwise(p, rows, base, up, down):
        s1, s2, s3, s4 = (sm[base + k * 128:base + k * 128 + 8, :] for k in range(4))
        level = lev[p + R, rows, :]
        im = img[p + R, rows, :]
        inner = s2 + EPS
        outer = 1.0 - s2 + EPS
        rest = s3 - s1
        both = inner * outer
        x1, x2 = s1 * outer, rest * inner
        spread = s4 - s3 * s3 + EPS
        force = (x1 - x2) * (2.0 * im * both - (x1 + x2)) / (both * both * spread * (np.pi * (1.0 + level * level)))
        lap = (lev[p + R + 1, rows, :] + lev[p + R - 1, rows, :] + up + down
               + pltpu.roll(level, 1, 1) + pltpu.roll(level, N - 1, 1) - 6.0 * level)
        out_ref[p, rows, :] = level + DT * (NU * lap + force)

    def inner_points(g):
        for o in range(G):
            p = g * G + o
            for s in range(8, 40, 8):
                pointwise(p, slice(s, s + 8), o * 32 + s - 8, lev[p + R, s + 1:s + 9, :], lev[p + R, s - 1:s + 7, :])

    sub = lax.broadcasted_iota(jnp.int32, (8, N), 0)

    def edge_points(e):
        for o in range(2 * G):
            p = e * 2 * G + o
            down = jnp.where(sub == 0, pltpu.roll(lev[p + R, YL:YL + 8, :], 1, 0), pltpu.roll(lev[p + R, 0:8, :], 1, 0))
            pointwise(p, slice(0, 8), o * 16, lev[p + R, 1:9, :], down)
            up = jnp.where(sub == 7, pltpu.roll(lev[p + R, YL + 8:YL + 16, :], 7, 0),
                           pltpu.roll(lev[p + R, 40:48, :], 7, 0))
            pointwise(p, slice(40, 48), o * 16 + 8, up, lev[p + R, 39:47, :])

    def inner(g):
        for chunk in range(3):
            smooth_z(g, chunk)
        smooth_y(g, t_yi, YL, 0)
        smooth_x()
        inner_points(g)

    def edge(e):
        for half in range(2):
            smooth_z(2 * e + half, 3)
            smooth_y(2 * e + half, t_ye, YE, half * 64)
        smooth_x()
        edge_points(e)

    even = lax.rem(col, 2) == 0
    near = jnp.where(even, 1, 0)
    far = 1 - near

    def arrived_side(side, *parts):
        for way, suffix in ((0, "above"), (1, "below")):
            @pl.when(side == way)
            def _():
                arrived(*(part + suffix for part in parts))

    for copy in own:
        copy.wait()
    fields(R, ZL, 0, YL, 16)

    @pl.loop(0, 4)
    def _(i):
        @pl.when(i == 2)
        def _():
            arrived_side(near, "")
            fields(near * (R + ZL), R, 0, YL, 16)

        inner(jnp.where(i < 2, i + 2, near * 4 + i - 2))

    arrived(("low", 0), ("low", 1), ("high", 0), ("high", 1))
    for name in ("corner above", "corner below"):
        for a in (0, 1):
            sent[name, a].start()
    arrived(("middle", 0), ("middle", 1))
    fields(R, ZL, YL, 16, 16)

    @pl.loop(0, 2)
    def _(i):
        @pl.when(i == 1)
        def _():
            arrived_side(near, "corner ")
            fields(near * (R + ZL), R, YL, 16, 16)

        edge(jnp.where(i == 0, 1, near * 2))

    arrived_side(far, "")
    fields(far * (R + ZL), R, 0, YL, 16)

    @pl.loop(0, 2)
    def _(i):
        inner(far * 4 + i)

    arrived_side(far, "corner ")
    fields(far * (R + ZL), R, YL, 16, 16)
    edge(far * 2)

    for copy in sent.values():
        copy.wait_send()


def step(level_set, image):
    consts = [jnp.asarray(t) for t in tables()]
    ext = pltpu.VMEM((ZE, YE, N), F32)
    half = pltpu.VMEM((4, ZL, YE, N), BF16)
    rows = 4 * G * 32
    return pl.pallas_call(
        kernel,
        out_shape=jax.ShapeDtypeStruct((ZL, YL, N), F32),
        in_specs=[pl.BlockSpec(memory_space=pltpu.HBM)] * 6,
        out_specs=pl.BlockSpec(memory_space=pltpu.VMEM),
        scratch_shapes=[ext] * 5 + [half, half, pltpu.VMEM((rows, N), BF16), pltpu.VMEM((rows, N), BF16),
                                    pltpu.VMEM((rows, N), F32)]
        + [pltpu.VMEM(c.shape, BF16) for c in consts]
        + [pltpu.SemaphoreType.DMA((8,)), pltpu.SemaphoreType.DMA((20,)), pltpu.SemaphoreType.DMA((20,))],
        compiler_params=pltpu.CompilerParams(
            collective_id=0, has_side_effects=True, vmem_limit_bytes=48 * 1024 * 1024),
    )(*[pltpu.with_memory_space_constraint(v, pltpu.HBM) for v in (level_set, image, *consts)])


def solution(mesh):
    return jax.shard_map(
        step,
        mesh=mesh,
        in_specs=(P("col", "row", None), P("col", "row", None)),
        out_specs=P("col", "row", None),
        check_vma=False,
    )
```

```python
import typing

import jax
import jax.numpy as jnp
import ml_dtypes
import numpy as np
from jax import lax
from jax.experimental import pallas as pl
from jax.experimental.pallas import tpu as pltpu
from jax.sharding import PartitionSpec as P

R = 6
N = 384
ZL, YL = 24, 48
ZE, YE = ZL + 2 * R, YL + 16
EPS = 0.05
SIGMA = 8.0
DT, NU = 0.5, 0.1
G = 4
F32, BF16 = jnp.float32, jnp.bfloat16
MESH = pl.DeviceIdType.MESH

ATAN = (
    0.3183096647262573, -0.10609224438667297, 0.06349188834428787, -0.044272541999816895,
    0.03069206140935421, -0.0177974384278059, 0.006959190126508474, -0.0012906072661280632,
)


class Part(typing.NamedTuple):
    plane: int
    planes: int
    start: int
    size: int


PARTS = {"low": Part(0, R, 0, 40), "high": Part(ZL - R, R, 40, 40), "middle": Part(R, ZL - 2 * R, 80, 72)}
PACKED = 152


def taps():
    offsets = np.arange(-R, R + 1, dtype=np.float64)
    weights = np.exp(-offsets * offsets / (2.0 * SIGMA * SIGMA))
    return weights / weights.sum()


def split(table):
    high = table.astype(np.float32).astype(ml_dtypes.bfloat16)
    low = (table - high.astype(np.float64)).astype(np.float32).astype(ml_dtypes.bfloat16)
    return high, low


def tables():
    weights = taps()

    def tap(distance):
        return weights[R + distance] if abs(distance) <= R else 0.0

    centre = weights[R]
    source = list(range(YL)) + list(range(-8, 0)) + list(range(YL, YL + 8))

    def block(outs, cols):
        one = np.array([[tap(source[c] - o) * centre for c in cols] for o in outs])
        return np.kron(np.eye(G), one)

    inner = block(range(8, 40), range(YL))
    edge = block(list(range(8)) + list(range(40, 48)), range(YE))
    i = np.arange(N)
    d = np.abs(i[:, None] - i[None, :])
    d = np.minimum(d, N - d)
    along_x = np.where(d <= R, weights[np.minimum(R + d, 2 * R)], 0.0)
    return tuple(np.concatenate(split(t)) for t in (inner, edge)) + split(along_x)


def heaviside(level):
    size = jnp.abs(level)
    big = size > 1.0
    t = jnp.where(big, 1.0 / jnp.maximum(size, 1.0), size)
    u = t * t
    q = jnp.full_like(u, ATAN[-1])
    for coeff in ATAN[-2::-1]:
        q = q * u + coeff
    q = q * t
    q = jnp.where(big, 0.5 - q, q)
    return 0.5 + jnp.where(level < 0.0, -q, q)


def kernel(level_hbm, image_hbm, y_in, y_ed, x_h, x_l, out_ref,
           lev, img, hv, hi, ii, g_h, g_l, xs_h, xs_l, sm,
           t_yi, t_ye, t_xh, t_xl,
           packed, halo, corner, local_sem, send_sem, recv_sem):
    row, col = lax.axis_index("row"), lax.axis_index("col")
    n_row, n_col = lax.axis_size("row"), lax.axis_size("col")
    r_up, r_dn = lax.rem(row + 1, n_row), lax.rem(row + n_row - 1, n_row)
    c_up, c_dn = lax.rem(col + 1, n_col), lax.rem(col + n_col - 1, n_col)

    barrier = pltpu.get_barrier_semaphore()
    for device in ({"row": row, "col": c_up}, {"row": row, "col": c_dn}, {"row": r_up, "col": col}, {"row": r_dn, "col": col}):
        pl.semaphore_signal(barrier, inc=1, device_id=device, device_id_type=MESH)

    own = []
    for i, (src, dst) in enumerate((
        (level_hbm, lev.at[R:R + ZL, 0:YL]), (image_hbm, img.at[R:R + ZL, 0:YL]),
        (y_in, t_yi), (y_ed, t_ye), (x_h, t_xh), (x_l, t_xl),
    )):
        copy = pltpu.make_async_copy(src, dst, local_sem.at[i])
        copy.start()
        own.append(copy)

    for block in (lev, img):
        block[:, YL:YE, :] = jnp.zeros((ZE, YE - YL, N), F32)
    for side in (0, 1):
        for a in (0, 1):
            for part in PARTS.values():
                if part.size > 6 * part.planes:
                    packed[side, a, part.start + 6 * part.planes:part.start + part.size, :] = jnp.zeros(
                        (part.size - 6 * part.planes, N), F32)

    def pack(part):
        for side, first in ((0, YL - R), (1, 0)):
            for a, block in enumerate((lev, img)):
                for q in range(part.planes):
                    at = part.start + 6 * q
                    packed[side, a, at:at + 6, :] = block[R + part.plane + q, first:first + 6, :]

    def unpack(src, start, planes, to):
        for side in (0, 1):
            for a, block in enumerate((lev, img)):
                for q in range(planes):
                    at = start + 6 * q
                    row0 = YL + 2 + 6 * side
                    block[to + q, row0:row0 + 6, :] = src[side, a, at:at + 6, :]

    sent = {}

    def send(name, axis, target, src, dst, now=True):
        i = len(sent)
        copy = pltpu.make_async_remote_copy(
            src_ref=src, dst_ref=dst, send_sem=send_sem.at[i], recv_sem=recv_sem.at[i],
            device_id={axis: target}, device_id_type=MESH,
        )
        if now:
            copy.start()
        sent[name] = copy

    def arrived(*names):
        for name in names:
            sent[name].wait_recv()

    def send_part(name):
        part = PARTS[name]
        rows = pl.ds(part.start, part.size)
        for side, target in ((0, r_up), (1, r_dn)):
            send((name, side), "row", target, packed.at[side, :, rows], halo.at[side, :, rows])

    own[0].wait()
    own[1].wait()
    pack(PARTS["low"])
    pack(PARTS["high"])
    pl.semaphore_wait(barrier, 4)
    send_part("low")
    send_part("high")
    pack(PARTS["middle"])
    send_part("middle")
    low, high, own_rows = pl.ds(0, R), pl.ds(ZL - R, R), pl.ds(0, YL)
    for a, (src, dst) in enumerate(((level_hbm, lev), (image_hbm, img))):
        send(("above", a), "col", c_up, src.at[high], dst.at[pl.ds(0, R), own_rows])
        send(("below", a), "col", c_dn, src.at[low], dst.at[pl.ds(R + ZL, R), own_rows])
    outer = {"corner above": (c_up, PARTS["high"], 0), "corner below": (c_dn, PARTS["low"], 1)}
    for name, (target, part, way) in outer.items():
        send(name, "col", target, halo.at[:, :, pl.ds(part.start, part.size)], corner.at[way], False)

    def fields(first, count, start, size, step):
        @pl.loop(first, first + count)
        def _(p):
            for s in range(start, start + size, step):
                rows = slice(s, s + step)
                h = heaviside(lev[p, rows, :])
                im = img[p, rows, :]
                hv[p, rows, :] = h
                hi[p, rows, :] = h * im
                ii[p, rows, :] = im * im

    weights = taps()
    ratio = [float(np.float32(weights[R + d] / weights[R])) for d in range(R + 1)]

    def smooth_z(g, chunk):
        rows = slice(chunk * 16, chunk * 16 + 16)
        for k, ref in enumerate((hi, hv, img, ii)):
            for lt in range(3):
                lanes = slice(lt * 128, lt * 128 + 128)
                f = [ref[g * G + j, rows, lanes] for j in range(G + 2 * R)]
                for o in range(G):
                    total = f[o + R]
                    for d in range(1, R + 1):
                        total = total + ratio[d] * (f[o + R - d] + f[o + R + d])
                    high = total.astype(BF16)
                    g_h[k, g * G + o, rows, lanes] = high
                    g_l[k, g * G + o, rows, lanes] = (total - high.astype(F32)).astype(BF16)

    def dot(a, b):
        return jnp.dot(a, b, preferred_element_type=F32)

    def smooth_y(g, table, depth, base):
        planes = pl.ds(g * G, G)
        m = table.shape[0] // 2
        for k in range(4):
            high = g_h[k, planes, 0:depth, :].reshape(G * depth, N)
            low = g_l[k, planes, 0:depth, :].reshape(G * depth, N)
            y = dot(table[...], high)
            y = y[0:m] + y[m:2 * m] + dot(table[0:m, :], low)
            yh = y.astype(BF16)
            xs_h[k * 128 + base:k * 128 + base + m, :] = yh
            xs_l[k * 128 + base:k * 128 + base + m, :] = (y - yh.astype(F32)).astype(BF16)

    def smooth_x():
        a = xs_h[...]
        sm[...] = dot(a, t_xh[...]) + dot(a, t_xl[...]) + dot(xs_l[...], t_xh[...])

    def pointwise(p, rows, base, up, down):
        s1, s2, s3, s4 = (sm[base + k * 128:base + k * 128 + 8, :] for k in range(4))
        level = lev[p + R, rows, :]
        im = img[p + R, rows, :]
        inner = s2 + EPS
        outer = 1.0 - s2 + EPS
        rest = s3 - s1
        both = inner * outer
        x1, x2 = s1 * outer, rest * inner
        spread = s4 - s3 * s3 + EPS
        force = (x1 - x2) * (2.0 * im * both - (x1 + x2)) / (both * both * spread * (np.pi * (1.0 + level * level)))
        lap = (lev[p + R + 1, rows, :] + lev[p + R - 1, rows, :] + up + down
               + pltpu.roll(level, 1, 1) + pltpu.roll(level, N - 1, 1) - 6.0 * level)
        out_ref[p, rows, :] = level + DT * (NU * lap + force)

    def inner_points(g):
        for o in range(G):
            p = g * G + o
            for s in range(8, 40, 8):
                pointwise(p, slice(s, s + 8), o * 32 + s - 8, lev[p + R, s + 1:s + 9, :], lev[p + R, s - 1:s + 7, :])

    sub = lax.broadcasted_iota(jnp.int32, (8, N), 0)

    def edge_points(e):
        for o in range(2 * G):
            p = e * 2 * G + o
            down = jnp.where(sub == 0, pltpu.roll(lev[p + R, YL:YL + 8, :], 1, 0), pltpu.roll(lev[p + R, 0:8, :], 1, 0))
            pointwise(p, slice(0, 8), o * 16, lev[p + R, 1:9, :], down)
            up = jnp.where(sub == 7, pltpu.roll(lev[p + R, YL + 8:YL + 16, :], 7, 0),
                           pltpu.roll(lev[p + R, 40:48, :], 7, 0))
            pointwise(p, slice(40, 48), o * 16 + 8, up, lev[p + R, 39:47, :])

    def inner(g):
        for chunk in range(3):
            smooth_z(g, chunk)
        smooth_y(g, t_yi, YL, 0)
        smooth_x()
        inner_points(g)

    def edge(e):
        for half in range(2):
            smooth_z(2 * e + half, 3)
            smooth_y(2 * e + half, t_ye, YE, half * 64)
        smooth_x()
        edge_points(e)

    even = lax.rem(col, 2) == 0
    near = jnp.where(even, 1, 0)
    far = 1 - near

    def z_halo(side):
        for way, name in ((0, "above"), (1, "below")):
            @pl.when(side == way)
            def _():
                arrived((name, 0), (name, 1))
        fields(side * (R + ZL), R, 0, YL, 16)

    def corner_halo(side):
        for way, name in ((0, "corner above"), (1, "corner below")):
            @pl.when(side == way)
            def _():
                arrived(name)
                unpack(corner.at[way], 0, R, way * (R + ZL))
        fields(side * (R + ZL), R, YL, 16, 16)

    fields(R, ZL, 0, YL, 16)
    for copy in own[2:]:
        copy.wait()

    @pl.loop(0, 4)
    def _(i):
        @pl.when(i == 2)
        def _():
            z_halo(near)

        inner(jnp.where(i < 2, i + 2, near * 4 + i - 2))

    arrived(("low", 0), ("low", 1), ("high", 0), ("high", 1))
    for name in outer:
        sent[name].start()
    arrived(("middle", 0), ("middle", 1))
    for part in PARTS.values():
        unpack(halo, part.start, part.planes, R + part.plane)
    fields(R, ZL, YL, 16, 16)

    @pl.loop(0, 2)
    def _(i):
        @pl.when(i == 1)
        def _():
            corner_halo(near)

        edge(jnp.where(i == 0, 1, near * 2))

    z_halo(far)

    @pl.loop(0, 2)
    def _(i):
        inner(far * 4 + i)

    corner_halo(far)
    edge(far * 2)

    for copy in sent.values():
        copy.wait_send()


def step(level_set, image):
    consts = [jnp.asarray(t) for t in tables()]
    ext = pltpu.VMEM((ZE, YE, N), F32)
    half = pltpu.VMEM((4, ZL, YE, N), BF16)
    rows = 4 * G * 32
    return pl.pallas_call(
        kernel,
        out_shape=jax.ShapeDtypeStruct((ZL, YL, N), F32),
        in_specs=[pl.BlockSpec(memory_space=pltpu.HBM)] * 6,
        out_specs=pl.BlockSpec(memory_space=pltpu.VMEM),
        scratch_shapes=[ext] * 5 + [half, half, pltpu.VMEM((rows, N), BF16), pltpu.VMEM((rows, N), BF16),
                                    pltpu.VMEM((rows, N), F32)]
        + [pltpu.VMEM(c.shape, BF16) for c in consts]
        + [pltpu.VMEM((2, 2, PACKED, N), F32)] * 2 + [pltpu.VMEM((2, 2, 2, 40, N), F32)]
        + [pltpu.SemaphoreType.DMA((8,)), pltpu.SemaphoreType.DMA((12,)), pltpu.SemaphoreType.DMA((12,))],
        compiler_params=pltpu.CompilerParams(
            collective_id=0, has_side_effects=True, vmem_limit_bytes=48 * 1024 * 1024),
    )(*[pltpu.with_memory_space_constraint(v, pltpu.HBM) for v in (level_set, image, *consts)])


def solution(mesh):
    return jax.shard_map(
        step,
        mesh=mesh,
        in_specs=(P("col", "row", None), P("col", "row", None)),
        out_specs=P("col", "row", None),
        check_vma=False,
    )
```

```python
import functools
import typing

import jax
import jax.numpy as jnp
import ml_dtypes
import numpy as np
from jax import lax
from jax.experimental import pallas as pl
from jax.experimental.pallas import tpu as pltpu
from jax.sharding import PartitionSpec as P

R = 6
N = 384
ZL, YL = 24, 48
ZE, YE = ZL + 2 * R, YL + 16
EPS = 0.05
SIGMA = 8.0
DT, NU = 0.5, 0.1
G = 4
F32, BF16 = jnp.float32, jnp.bfloat16
MESH = pl.DeviceIdType.MESH

ATAN = (
    0.3183096647262573, -0.10609224438667297, 0.06349188834428787, -0.044272541999816895,
    0.03069206140935421, -0.0177974384278059, 0.006959190126508474, -0.0012906072661280632,
)


class Part(typing.NamedTuple):
    plane: int
    planes: int
    start: int
    size: int


PARTS = {"low": Part(0, R, 0, 40), "high": Part(ZL - R, R, 40, 40), "middle": Part(R, ZL - 2 * R, 80, 72)}
PACKED = 152
WINDOWS = (-32, 160)


def taps():
    offsets = np.arange(-R, R + 1, dtype=np.float64)
    weights = np.exp(-offsets * offsets / (2.0 * SIGMA * SIGMA))
    return weights / weights.sum()


def split(table):
    high = table.astype(np.float32).astype(ml_dtypes.bfloat16)
    low = (table - high.astype(np.float64)).astype(np.float32).astype(ml_dtypes.bfloat16)
    return high, low


def tables():
    weights = taps()

    def tap(distance):
        return weights[R + distance] if abs(distance) <= R else 0.0

    centre = weights[R]
    source = list(range(YL)) + list(range(-8, 0)) + list(range(YL, YL + 8))

    def block(outs, cols):
        one = np.array([[tap(source[c] - o) * centre for c in cols] for o in outs])
        return np.kron(np.eye(G), one)

    inner = block(range(8, 40), range(YL))
    edge = block(list(range(8)) + list(range(40, 48)), range(YE))
    halves = []
    for start, first, outs in ((WINDOWS[0], 0, range(0, N // 2)), (WINDOWS[1], 128, range(N // 2, N))):
        half = np.zeros((256, 256))
        for o in outs:
            for d in range(-R, R + 1):
                half[o + d - start, o - first] = weights[R + d]
        high, low = split(half)
        halves.append(np.concatenate([high, high, low]))
    return tuple(np.concatenate(split(t)) for t in (inner, edge)) + (np.stack(halves),)


def heaviside(level):
    size = jnp.abs(level)
    big = size > 1.0
    t = jnp.where(big, 1.0 / jnp.maximum(size, 1.0), size)
    u = t * t
    q = jnp.full_like(u, ATAN[-1])
    for coeff in ATAN[-2::-1]:
        q = q * u + coeff
    q = q * t
    q = jnp.where(big, 0.5 - q, q)
    return 0.5 + jnp.where(level < 0.0, -q, q)


def kernel(level_hbm, image_hbm, y_in, y_ed, x_all, out_ref,
           lev, img, hv, hi, ii, g_h, g_l, xs_h, xs_l, sm,
           t_yi, t_ye, t_x,
           packed, halo, corner, relay, local_sem, send_sem, recv_sem):
    row, col = lax.axis_index("row"), lax.axis_index("col")
    n_row, n_col = lax.axis_size("row"), lax.axis_size("col")
    r_up, r_dn = lax.rem(row + 1, n_row), lax.rem(row + n_row - 1, n_row)
    c_up, c_dn = lax.rem(col + 1, n_col), lax.rem(col + n_col - 1, n_col)

    barrier = pltpu.get_barrier_semaphore()
    for device in ({"row": row, "col": c_up}, {"row": row, "col": c_dn}, {"row": r_up, "col": col}, {"row": r_dn, "col": col}):
        pl.semaphore_signal(barrier, inc=1, device_id=device, device_id_type=MESH)

    own = []
    for i, (src, dst) in enumerate((
        (level_hbm, lev.at[R:R + ZL, 0:YL]), (image_hbm, img.at[R:R + ZL, 0:YL]),
        (y_in, t_yi), (y_ed, t_ye), (x_all, t_x),
    )):
        copy = pltpu.make_async_copy(src, dst, local_sem.at[i])
        copy.start()
        own.append(copy)

    for block in (lev, img):
        block[:, YL:YE, :] = jnp.zeros((ZE, YE - YL, N), F32)
    for side in (0, 1):
        for a in (0, 1):
            for part in PARTS.values():
                if part.size > 6 * part.planes:
                    packed[side, a, part.start + 6 * part.planes:part.start + part.size, :] = jnp.zeros(
                        (part.size - 6 * part.planes, N), F32)

    def pack(part):
        for side, first in ((0, YL - R), (1, 0)):
            for a, block in enumerate((lev, img)):
                for q in range(part.planes):
                    at = part.start + 6 * q
                    packed[side, a, at:at + 6, :] = block[R + part.plane + q, first:first + 6, :]

    def unpack(src, start, planes, to):
        for side in (0, 1):
            for a, block in enumerate((lev, img)):
                for q in range(planes):
                    at = start + 6 * q
                    row0 = YL + 2 + 6 * side
                    block[to + q, row0:row0 + 6, :] = src[side, a, at:at + 6, :]

    sent, slots = {}, {}

    def send(name, axis, target, src, dst, now=True, lands=None):
        i = len(sent)
        slots[name] = i if lands is None else slots[lands]
        copy = pltpu.make_async_remote_copy(
            src_ref=src, dst_ref=dst, send_sem=send_sem.at[i], recv_sem=recv_sem.at[slots[name]],
            device_id={axis: target}, device_id_type=MESH,
        )
        if now:
            copy.start()
        sent[name] = copy

    def arrived(*names):
        for name in names:
            sent[name].wait_recv()

    def send_part(name):
        part = PARTS[name]
        rows = pl.ds(part.start, part.size)
        for side, target in ((0, r_up), (1, r_dn)):
            send((name, side), "row", target, packed.at[side, :, rows], halo.at[side, :, rows])

    other = row + 1 - 2 * lax.rem(row, 2)
    outer_row = jnp.logical_or(lax.rem(row, 4) == 0, lax.rem(row, 4) == 3)
    wraps = (lax.rem(col, 8) == 7, lax.rem(col, 8) == 0)
    corner_way = [jnp.logical_and(outer_row, w) for w in wraps]
    helper_way = [jnp.logical_and(jnp.logical_not(outer_row), w) for w in wraps]
    arrays = ((level_hbm, lev), (image_hbm, img))
    upper, lower = pl.ds(0, 24), pl.ds(24, 24)
    z_ways = ((c_up, ZL - 2, R - 2, ZL - R, 0), (c_dn, 0, R + ZL, 2, R + ZL + 2))
    for way, (target, two, two_to, four, four_to) in enumerate(z_ways):
        for a, (src, dst) in enumerate(arrays):
            send(("two", way, a), "col", target, src.at[pl.ds(two, 2)], dst.at[pl.ds(two_to, 2), pl.ds(0, YL)], False)
            for name, rows in (("upper", upper), ("lower", lower)):
                send((name, way, a), "col", target, src.at[pl.ds(four, 4), rows], dst.at[pl.ds(four_to, 4), rows], False)
            send(("first", way, a), "row", other, src.at[pl.ds(four, 4), lower], relay.at[0, a], False,
                 ("first", 0, a) if way else None)
        send(("second", way), "col", target, relay.at[0], relay.at[1], False, ("second", 0) if way else None)
    for way, (_, _, _, _, four_to) in enumerate(z_ways):
        for a, (_, dst) in enumerate(arrays):
            send(("third", way, a), "row", other, relay.at[1, a], dst.at[pl.ds(four_to, 4), lower], False,
                 ("lower", way, a))

    def start(*names):
        for name in names:
            sent[name].start()

    def by_way(predicates, action):
        for way in (0, 1):
            pl.when(predicates[way])(functools.partial(action, way))

    own[0].wait()
    own[1].wait()
    pack(PARTS["low"])
    pack(PARTS["high"])
    pl.semaphore_wait(barrier, 4)
    by_way(corner_way, lambda way: start(("first", way, 0), ("first", way, 1)))
    send_part("low")
    send_part("high")
    pack(PARTS["middle"])
    send_part("middle")
    start(*[("two", way, a) for way in (0, 1) for a in (0, 1)])
    direct_way = [jnp.logical_not(p) for p in corner_way]
    upper_now = [jnp.logical_not(p) for p in helper_way]
    lower_now = [jnp.logical_not(jnp.logical_or(p, q)) for p, q in zip(corner_way, helper_way)]
    by_way(upper_now, lambda way: start(("upper", way, 0), ("upper", way, 1)))
    by_way(lower_now, lambda way: start(("lower", way, 0), ("lower", way, 1)))

    def forward(way):
        arrived(("first", 0, 0), ("first", 0, 1))
        start(("second", way), *[(name, way, a) for name in ("upper", "lower") for a in (0, 1)])

    def deliver(way):
        arrived(("second", 0))
        start(("third", 1 - way, 0), ("third", 1 - way, 1))

    outer = {"corner above": (c_up, PARTS["high"], 0), "corner below": (c_dn, PARTS["low"], 1)}
    for name, (target, part, way) in outer.items():
        send(name, "col", target, halo.at[:, :, pl.ds(part.start, part.size)], corner.at[way], False)

    def fields(first, count, start, size, step):
        @pl.loop(first, first + count)
        def _(p):
            for s in range(start, start + size, step):
                rows = slice(s, s + step)
                h = heaviside(lev[p, rows, :])
                im = img[p, rows, :]
                hv[p, rows, :] = h
                hi[p, rows, :] = h * im
                ii[p, rows, :] = im * im

    weights = taps()
    ratio = [float(np.float32(weights[R + d] / weights[R])) for d in range(R + 1)]

    def smooth_z(g, chunk):
        rows = slice(chunk * 16, chunk * 16 + 16)
        for k, ref in enumerate((hi, hv, img, ii)):
            for lt in range(3):
                lanes = slice(lt * 128, lt * 128 + 128)
                f = [ref[g * G + j, rows, lanes] for j in range(G + 2 * R)]
                for o in range(G):
                    total = f[o + R]
                    for d in range(1, R + 1):
                        total = total + ratio[d] * (f[o + R - d] + f[o + R + d])
                    high = total.astype(BF16)
                    g_h[k, g * G + o, rows, lanes] = high
                    g_l[k, g * G + o, rows, lanes] = (total - high.astype(F32)).astype(BF16)

    def dot(a, b):
        return jnp.dot(a, b, preferred_element_type=F32)

    def smooth_y(g, table, depth, base):
        planes = pl.ds(g * G, G)
        m = table.shape[0] // 2
        high = [g_h[k, planes, 0:depth, :].reshape(G * depth, N) for k in range(4)]
        low = [g_l[k, planes, 0:depth, :].reshape(G * depth, N) for k in range(4)]
        for k in range(0, 4, 2):
            pair = dot(table[...], jnp.concatenate(high[k:k + 2], axis=1))
            pair = pair[0:m] + pair[m:2 * m] + dot(table[0:m, :], jnp.concatenate(low[k:k + 2], axis=1))
            for f in (0, 1):
                y = pair[:, f * N:(f + 1) * N]
                rows = slice((k + f) * 128 + base, (k + f) * 128 + base + m)
                for w, start in enumerate(WINDOWS):
                    part = pltpu.roll(y, -start % N, 1)[:, 0:256]
                    ph = part.astype(BF16)
                    xs_h[w, rows, :] = ph
                    xs_l[w, rows, :] = (part - ph.astype(F32)).astype(BF16)

    def smooth_x():
        for w in (0, 1):
            a = xs_h[w]
            part = dot(jnp.concatenate([a, xs_l[w], a], axis=1), t_x[w])
            if w == 0:
                sm[:, 0:256] = part
            else:
                sm[:, 128:256] = sm[:, 128:256] + part[:, 0:128]
                sm[:, 256:384] = part[:, 128:256]

    def pointwise(p, rows, base, up, down):
        s1, s2, s3, s4 = (sm[base + k * 128:base + k * 128 + 8, :] for k in range(4))
        level = lev[p + R, rows, :]
        im = img[p + R, rows, :]
        inner = s2 + EPS
        outer = 1.0 - s2 + EPS
        rest = s3 - s1
        both = inner * outer
        x1, x2 = s1 * outer, rest * inner
        spread = s4 - s3 * s3 + EPS
        force = (x1 - x2) * (2.0 * im * both - (x1 + x2)) / (both * both * spread * (np.pi * (1.0 + level * level)))
        lap = (lev[p + R + 1, rows, :] + lev[p + R - 1, rows, :] + up + down
               + pltpu.roll(level, 1, 1) + pltpu.roll(level, N - 1, 1) - 6.0 * level)
        out_ref[p, rows, :] = level + DT * (NU * lap + force)

    def inner_points(g):
        for o in range(G):
            p = g * G + o
            for s in range(8, 40, 8):
                pointwise(p, slice(s, s + 8), o * 32 + s - 8, lev[p + R, s + 1:s + 9, :], lev[p + R, s - 1:s + 7, :])

    sub = lax.broadcasted_iota(jnp.int32, (8, N), 0)

    def edge_points(e):
        for o in range(2 * G):
            p = e * 2 * G + o
            down = jnp.where(sub == 0, pltpu.roll(lev[p + R, YL:YL + 8, :], 1, 0), pltpu.roll(lev[p + R, 0:8, :], 1, 0))
            pointwise(p, slice(0, 8), o * 16, lev[p + R, 1:9, :], down)
            up = jnp.where(sub == 7, pltpu.roll(lev[p + R, YL + 8:YL + 16, :], 7, 0),
                           pltpu.roll(lev[p + R, 40:48, :], 7, 0))
            pointwise(p, slice(40, 48), o * 16 + 8, up, lev[p + R, 39:47, :])

    def inner(g):
        for chunk in range(3):
            smooth_z(g, chunk)
        smooth_y(g, t_yi, YL, 0)
        smooth_x()
        inner_points(g)

    def edge(e):
        for half in range(2):
            smooth_z(2 * e + half, 3)
            smooth_y(2 * e + half, t_ye, YE, half * 64)
        smooth_x()
        edge_points(e)

    even = lax.rem(col, 2) == 0
    near = jnp.where(even, 1, 0)
    far = 1 - near

    def z_arrived(side, *names):
        by_way((side == 0, side == 1), lambda way: arrived(*[(name, way, a) for name in names for a in (0, 1)]))

    def corner_halo(side):
        for way, name in ((0, "corner above"), (1, "corner below")):
            @pl.when(side == way)
            def _():
                arrived(name)
                unpack(corner.at[way], 0, R, way * (R + ZL))
        fields(side * (R + ZL), R, YL, 16, 16)

    fields(R, ZL, 0, YL, 16)
    for copy in own[2:]:
        copy.wait()

    @pl.loop(0, 4)
    def _(i):
        @pl.when(i == 1)
        def _():
            by_way(helper_way, forward)

        @pl.when(i == 2)
        def _():
            z_arrived(near, "two", "upper", "lower")
            fields(near * (R + ZL), R, 0, YL, 16)

        inner(jnp.where(i < 2, i + 2, near * 4 + i - 2))

    by_way(helper_way, deliver)

    arrived(("low", 0), ("low", 1), ("high", 0), ("high", 1))
    for name in outer:
        sent[name].start()
    arrived(("middle", 0), ("middle", 1))
    for part in PARTS.values():
        unpack(halo, part.start, part.planes, R + part.plane)
    fields(R, ZL, YL, 16, 16)

    @pl.loop(0, 2)
    def _(i):
        @pl.when(i == 1)
        def _():
            corner_halo(near)

        edge(jnp.where(i == 0, 1, near * 2))

    @pl.loop(0, 2)
    def _(i):
        @pl.when(i == 0)
        def _():
            z_arrived(far, "two")
            fields(far * (R + ZL - 4) + 4, 2, 0, YL, 16)

        @pl.when(i == 1)
        def _():
            z_arrived(far, "upper", "lower")
            fields(far * (R + ZL + 2), 4, 0, YL, 16)

        inner(jnp.where(i == 0, 1 + 3 * far, 5 * far))

    corner_halo(far)
    edge(far * 2)

    def all_sent(*names):
        for name in names:
            sent[name].wait_send()

    held = ("lower", "first", "second", "third")
    all_sent(*[name for name in sent if name[0] not in held])
    by_way(direct_way, lambda way: all_sent(("lower", way, 0), ("lower", way, 1)))
    by_way(corner_way, lambda way: all_sent(("first", way, 0), ("first", way, 1)))
    by_way(helper_way, lambda way: all_sent(("second", way), ("third", 1 - way, 0), ("third", 1 - way, 1)))


def step(level_set, image):
    consts = [jnp.asarray(t) for t in tables()]
    ext = pltpu.VMEM((ZE, YE, N), F32)
    half = pltpu.VMEM((4, ZL, YE, N), BF16)
    rows = 4 * G * 32
    return pl.pallas_call(
        kernel,
        out_shape=jax.ShapeDtypeStruct((ZL, YL, N), F32),
        in_specs=[pl.BlockSpec(memory_space=pltpu.HBM)] * 5,
        out_specs=pl.BlockSpec(memory_space=pltpu.VMEM),
        scratch_shapes=[ext] * 5 + [half, half, pltpu.VMEM((2, rows, 256), BF16), pltpu.VMEM((2, rows, 256), BF16),
                                    pltpu.VMEM((rows, N), F32)]
        + [pltpu.VMEM(c.shape, BF16) for c in consts]
        + [pltpu.VMEM((2, 2, PACKED, N), F32)] * 2 + [pltpu.VMEM((2, 2, 2, 40, N), F32), pltpu.VMEM((2, 2, 4, 24, N), F32)]
        + [pltpu.SemaphoreType.DMA((8,)), pltpu.SemaphoreType.DMA((40,)), pltpu.SemaphoreType.DMA((40,))],
        compiler_params=pltpu.CompilerParams(
            collective_id=0, has_side_effects=True, vmem_limit_bytes=48 * 1024 * 1024),
    )(*[pltpu.with_memory_space_constraint(v, pltpu.HBM) for v in (level_set, image, *consts)])


def solution(mesh):
    return jax.shard_map(
        step,
        mesh=mesh,
        in_specs=(P("col", "row", None), P("col", "row", None)),
        out_specs=P("col", "row", None),
        check_vma=False,
    )
```

```python
import functools
import typing

import jax
import jax.numpy as jnp
import ml_dtypes
import numpy as np
from jax import lax
from jax.experimental import pallas as pl
from jax.experimental.pallas import tpu as pltpu
from jax.sharding import PartitionSpec as P

R = 6
N = 384
ZL, YL = 24, 48
ZE, YE = ZL + 2 * R, YL + 16
EPS = 0.05
SIGMA = 8.0
DT, NU = 0.5, 0.1
G = 4
F32, BF16 = jnp.float32, jnp.bfloat16
MESH = pl.DeviceIdType.MESH

ATAN = (
    0.3183096647262573, -0.10609224438667297, 0.06349188834428787, -0.044272541999816895,
    0.03069206140935421, -0.0177974384278059, 0.006959190126508474, -0.0012906072661280632,
)


class Part(typing.NamedTuple):
    plane: int
    planes: int
    start: int
    size: int


PARTS = {"low": Part(0, R, 0, 40), "high": Part(ZL - R, R, 40, 40), "middle": Part(R, ZL - 2 * R, 80, 72)}
PACKED = 152
WINDOWS = (-32, 160)


def taps():
    offsets = np.arange(-R, R + 1, dtype=np.float64)
    weights = np.exp(-offsets * offsets / (2.0 * SIGMA * SIGMA))
    return weights / weights.sum()


def split(table):
    high = table.astype(np.float32).astype(ml_dtypes.bfloat16)
    low = (table - high.astype(np.float64)).astype(np.float32).astype(ml_dtypes.bfloat16)
    return high, low


def tables():
    weights = taps()

    def tap(distance):
        return weights[R + distance] if abs(distance) <= R else 0.0

    centre = weights[R]
    source = list(range(YL)) + list(range(-8, 0)) + list(range(YL, YL + 8))

    def block(outs, cols):
        one = np.array([[tap(source[c] - o) * centre for c in cols] for o in outs])
        return np.kron(np.eye(G), one)

    inner = block(range(8, 40), range(YL))
    edge = block(list(range(8)) + list(range(40, 48)), range(YE))
    halves = []
    for start, first, outs in ((WINDOWS[0], 0, range(0, N // 2)), (WINDOWS[1], 128, range(N // 2, N))):
        half = np.zeros((256, 256))
        for o in outs:
            for d in range(-R, R + 1):
                half[o + d - start, o - first] = weights[R + d]
        high, low = split(half)
        halves.append(np.concatenate([high, high, low]))
    return tuple(np.concatenate(split(t)) for t in (inner, edge)) + (np.stack(halves),)


def heaviside(level):
    big = jnp.abs(level) > 1.0
    t = jnp.where(big, 1.0 / jnp.where(big, level, 1.0), level)
    u = t * t
    q = jnp.full_like(u, ATAN[-1])
    for coeff in ATAN[-2::-1]:
        q = q * u + coeff
    q = q * t
    return jnp.where(big, jnp.where(level > 0.0, 1.0, 0.0) - q, 0.5 + q)


def kernel(level_hbm, image_hbm, y_in, y_ed, x_all, out_ref,
           lev, img, hv, hi, ii, g_h, g_l, xs_h, xs_l, sm,
           t_yi, t_ye, t_x,
           packed, halo, corner, relay, local_sem, send_sem, recv_sem):
    row, col = lax.axis_index("row"), lax.axis_index("col")
    n_row, n_col = lax.axis_size("row"), lax.axis_size("col")
    r_up, r_dn = lax.rem(row + 1, n_row), lax.rem(row + n_row - 1, n_row)
    c_up, c_dn = lax.rem(col + 1, n_col), lax.rem(col + n_col - 1, n_col)

    barrier = pltpu.get_barrier_semaphore()
    for device in ({"row": row, "col": c_up}, {"row": row, "col": c_dn}, {"row": r_up, "col": col}, {"row": r_dn, "col": col}):
        pl.semaphore_signal(barrier, inc=1, device_id=device, device_id_type=MESH)

    own = []
    for i, (src, dst) in enumerate((
        (level_hbm, lev.at[R:R + ZL, 0:YL]), (image_hbm, img.at[R:R + ZL, 0:YL]),
        (y_in, t_yi), (y_ed, t_ye), (x_all, t_x),
    )):
        copy = pltpu.make_async_copy(src, dst, local_sem.at[i])
        copy.start()
        own.append(copy)

    for side in (0, 1):
        for a in (0, 1):
            for part in PARTS.values():
                if part.size > 6 * part.planes:
                    packed[side, a, part.start + 6 * part.planes:part.start + part.size, :] = jnp.zeros(
                        (part.size - 6 * part.planes, N), F32)

    def pack(part):
        for side, first in ((0, YL - R), (1, 0)):
            for a, block in enumerate((lev, img)):
                for q in range(part.planes):
                    at = part.start + 6 * q
                    packed[side, a, at:at + 6, :] = block[R + part.plane + q, first:first + 6, :]

    def unpack(src, start, planes, to):
        for side in (0, 1):
            for a, block in enumerate((lev, img)):
                for q in range(planes):
                    at = start + 6 * q
                    row0 = YL + 2 + 6 * side
                    block[to + q, row0:row0 + 6, :] = src[side, a, at:at + 6, :]

    sent, slots = {}, {}

    def send(name, axis, target, src, dst, now=True, lands=None):
        i = len(sent)
        slots[name] = i if lands is None else slots[lands]
        copy = pltpu.make_async_remote_copy(
            src_ref=src, dst_ref=dst, send_sem=send_sem.at[i], recv_sem=recv_sem.at[slots[name]],
            device_id={axis: target}, device_id_type=MESH,
        )
        if now:
            copy.start()
        sent[name] = copy

    def arrived(*names):
        for name in names:
            sent[name].wait_recv()

    def send_part(name):
        part = PARTS[name]
        rows = pl.ds(part.start, part.size)
        for side, target in ((0, r_up), (1, r_dn)):
            send((name, side), "row", target, packed.at[side, :, rows], halo.at[side, :, rows])

    other = row + 1 - 2 * lax.rem(row, 2)
    outer_row = jnp.logical_or(lax.rem(row, 4) == 0, lax.rem(row, 4) == 3)
    wraps = (lax.rem(col, 8) == 7, lax.rem(col, 8) == 0)
    corner_way = [jnp.logical_and(outer_row, w) for w in wraps]
    helper_way = [jnp.logical_and(jnp.logical_not(outer_row), w) for w in wraps]
    arrays = ((level_hbm, lev), (image_hbm, img))
    upper, lower = pl.ds(0, 24), pl.ds(24, 24)
    z_ways = ((c_up, ZL - 2, R - 2, ZL - R, 0), (c_dn, 0, R + ZL, 2, R + ZL + 2))
    for way, (target, two, two_to, four, four_to) in enumerate(z_ways):
        for a, (src, dst) in enumerate(arrays):
            send(("two", way, a), "col", target, src.at[pl.ds(two, 2)], dst.at[pl.ds(two_to, 2), pl.ds(0, YL)], False)
            for name, rows in (("upper", upper), ("lower", lower)):
                send((name, way, a), "col", target, src.at[pl.ds(four, 4), rows], dst.at[pl.ds(four_to, 4), rows], False)
            send(("first", way, a), "row", other, src.at[pl.ds(four, 4), lower], relay.at[0, a], False,
                 ("first", 0, a) if way else None)
        send(("second", way), "col", target, relay.at[0], relay.at[1], False, ("second", 0) if way else None)
    for way, (_, _, _, _, four_to) in enumerate(z_ways):
        for a, (_, dst) in enumerate(arrays):
            send(("third", way, a), "row", other, relay.at[1, a], dst.at[pl.ds(four_to, 4), lower], False,
                 ("lower", way, a))

    def start(*names):
        for name in names:
            sent[name].start()

    def by_way(predicates, action):
        for way in (0, 1):
            pl.when(predicates[way])(functools.partial(action, way))

    own[0].wait()
    own[1].wait()
    pack(PARTS["low"])
    pack(PARTS["high"])
    pl.semaphore_wait(barrier, 4)
    by_way(corner_way, lambda way: start(("first", way, 0), ("first", way, 1)))
    send_part("low")
    send_part("high")
    pack(PARTS["middle"])
    send_part("middle")
    start(*[("two", way, a) for way in (0, 1) for a in (0, 1)])
    direct_way = [jnp.logical_not(p) for p in corner_way]
    upper_now = [jnp.logical_not(p) for p in helper_way]
    lower_now = [jnp.logical_not(jnp.logical_or(p, q)) for p, q in zip(corner_way, helper_way)]
    by_way(upper_now, lambda way: start(("upper", way, 0), ("upper", way, 1)))
    by_way(lower_now, lambda way: start(("lower", way, 0), ("lower", way, 1)))

    def forward(way):
        arrived(("first", 0, 0), ("first", 0, 1))
        start(("second", way), *[(name, way, a) for name in ("upper", "lower") for a in (0, 1)])

    def deliver(way):
        arrived(("second", 0))
        start(("third", 1 - way, 0), ("third", 1 - way, 1))

    outer = {"corner above": (c_up, PARTS["high"], 0), "corner below": (c_dn, PARTS["low"], 1)}
    for name, (target, part, way) in outer.items():
        send(name, "col", target, halo.at[:, :, pl.ds(part.start, part.size)], corner.at[way], False)

    def fields(first, count, start, size, step):
        @pl.loop(0, count // 2)
        def _(i):
            planes = pl.ds(first + 2 * i, 2)
            for s in range(start, start + size, step):
                rows = slice(s, s + step)
                h = heaviside(lev[planes, rows, :])
                im = img[planes, rows, :]
                hv[planes, rows, :] = h
                hi[planes, rows, :] = h * im
                ii[planes, rows, :] = im * im

    weights = taps()
    ratio = [float(np.float32(weights[R + d] / weights[R])) for d in range(R + 1)]

    def smooth_z(g, chunk):
        rows = slice(chunk * 16, chunk * 16 + 16)
        waiting = []

        def store():
            for k, o, lanes, high, low in waiting:
                g_h[k, g * G + o, rows, lanes] = high
                g_l[k, g * G + o, rows, lanes] = low
            waiting.clear()

        for k, ref in enumerate((hi, hv, img, ii)):
            for lt in range(3):
                lanes = slice(lt * 128, lt * 128 + 128)
                f = [ref[g * G + j, rows, lanes] for j in range(G + 2 * R)]
                store()
                for o in range(G):
                    total = f[o + R]
                    for d in range(1, R + 1):
                        total = total + ratio[d] * (f[o + R - d] + f[o + R + d])
                    high = total.astype(BF16)
                    waiting.append((k, o, lanes, high, (total - high.astype(F32)).astype(BF16)))
        store()

    def dot(a, b):
        return jnp.dot(a, b, preferred_element_type=F32)

    def smooth_y(g, table, depth, base):
        planes = pl.ds(g * G, G)
        m = table.shape[0] // 2
        high = [g_h[k, planes, 0:depth, :].reshape(G * depth, N) for k in range(4)]
        low = [g_l[k, planes, 0:depth, :].reshape(G * depth, N) for k in range(4)]
        for k in range(0, 4, 2):
            pair = dot(table[...], jnp.concatenate(high[k:k + 2], axis=1))
            pair = pair[0:m] + pair[m:2 * m] + dot(table[0:m, :], jnp.concatenate(low[k:k + 2], axis=1))
            for f in (0, 1):
                y = pair[:, f * N:(f + 1) * N]
                rows = slice((k + f) * 128 + base, (k + f) * 128 + base + m)
                for w, start in enumerate(WINDOWS):
                    part = pltpu.roll(y, -start % N, 1)[:, 0:256]
                    ph = part.astype(BF16)
                    xs_h[w, rows, :] = ph
                    xs_l[w, rows, :] = (part - ph.astype(F32)).astype(BF16)

    def smooth_x():
        for w in (0, 1):
            a = xs_h[w]
            part = dot(jnp.concatenate([a, xs_l[w], a], axis=1), t_x[w])
            if w == 0:
                sm[:, 0:256] = part
            else:
                sm[:, 128:256] = sm[:, 128:256] + part[:, 0:128]
                sm[:, 256:384] = part[:, 128:256]

    def pointwise(p, rows, base, up, down):
        s1, s2, s3, s4 = (sm[base + k * 128:base + k * 128 + 8, :] for k in range(4))
        level = lev[p + R, rows, :]
        im = img[p + R, rows, :]
        inner = s2 + EPS
        outer = 1.0 - s2 + EPS
        rest = s3 - s1
        both = inner * outer
        x1, x2 = s1 * outer, rest * inner
        spread = s4 - s3 * s3 + EPS
        force = (x1 - x2) * (2.0 * im * both - (x1 + x2)) / (both * both * spread * (np.pi * (1.0 + level * level)))
        lap = (lev[p + R + 1, rows, :] + lev[p + R - 1, rows, :] + up + down
               + pltpu.roll(level, 1, 1) + pltpu.roll(level, N - 1, 1) - 6.0 * level)
        return level + DT * (NU * lap + force)

    def inner_points(g):
        for o in range(G):
            p = g * G + o
            for s in range(8, 40, 16):
                done = [pointwise(p, slice(t, t + 8), o * 32 + t - 8, lev[p + R, t + 1:t + 9, :], lev[p + R, t - 1:t + 7, :])
                        for t in (s, s + 8)]
                for t, value in zip((s, s + 8), done):
                    out_ref[p, t:t + 8, :] = value

    sub = lax.broadcasted_iota(jnp.int32, (8, N), 0)

    def edge_points(e):
        for o in range(2 * G):
            p = e * 2 * G + o
            down = jnp.where(sub == 0, pltpu.roll(lev[p + R, YL:YL + 8, :], 1, 0), pltpu.roll(lev[p + R, 0:8, :], 1, 0))
            up = jnp.where(sub == 7, pltpu.roll(lev[p + R, YL + 8:YL + 16, :], 7, 0),
                           pltpu.roll(lev[p + R, 40:48, :], 7, 0))
            first = pointwise(p, slice(0, 8), o * 16, lev[p + R, 1:9, :], down)
            last = pointwise(p, slice(40, 48), o * 16 + 8, up, lev[p + R, 39:47, :])
            out_ref[p, 0:8, :] = first
            out_ref[p, 40:48, :] = last

    def inner(g):
        for chunk in range(3):
            smooth_z(g, chunk)
        smooth_y(g, t_yi, YL, 0)
        smooth_x()
        inner_points(g)

    def edge(e):
        for half in range(2):
            smooth_z(2 * e + half, 3)
            smooth_y(2 * e + half, t_ye, YE, half * 64)
        smooth_x()
        edge_points(e)

    even = lax.rem(col, 2) == 0
    near = jnp.where(even, 1, 0)
    far = 1 - near

    def z_arrived(side, *names):
        by_way((side == 0, side == 1), lambda way: arrived(*[(name, way, a) for name in names for a in (0, 1)]))

    def corner_halo(side):
        for way, name in ((0, "corner above"), (1, "corner below")):
            @pl.when(side == way)
            def _():
                arrived(name)
                unpack(corner.at[way], 0, R, way * (R + ZL))
        fields(side * (R + ZL), R, YL, 16, 16)

    for block in (lev, img):
        block[:, YL:YE, :] = jnp.zeros((ZE, YE - YL, N), F32)
    fields(R, ZL, 0, YL, 16)
    for copy in own[2:]:
        copy.wait()

    @pl.loop(0, 4)
    def _(i):
        @pl.when(i == 1)
        def _():
            by_way(helper_way, forward)

        @pl.when(i == 2)
        def _():
            z_arrived(near, "two", "upper", "lower")
            fields(near * (R + ZL), R, 0, YL, 16)

        inner(jnp.where(i < 2, i + 2, near * 4 + i - 2))

    by_way(helper_way, deliver)

    arrived(("low", 0), ("low", 1), ("high", 0), ("high", 1))
    for name in outer:
        sent[name].start()
    arrived(("middle", 0), ("middle", 1))
    for part in PARTS.values():
        unpack(halo, part.start, part.planes, R + part.plane)
    fields(R, ZL, YL, 16, 16)

    @pl.loop(0, 2)
    def _(i):
        @pl.when(i == 1)
        def _():
            corner_halo(near)

        edge(jnp.where(i == 0, 1, near * 2))

    @pl.loop(0, 2)
    def _(i):
        @pl.when(i == 0)
        def _():
            z_arrived(far, "two")
            fields(far * (R + ZL - 4) + 4, 2, 0, YL, 16)

        @pl.when(i == 1)
        def _():
            z_arrived(far, "upper", "lower")
            fields(far * (R + ZL + 2), 4, 0, YL, 16)

        inner(jnp.where(i == 0, 1 + 3 * far, 5 * far))

    corner_halo(far)
    edge(far * 2)

    def all_sent(*names):
        for name in names:
            sent[name].wait_send()

    held = ("lower", "first", "second", "third")
    all_sent(*[name for name in sent if name[0] not in held])
    by_way(direct_way, lambda way: all_sent(("lower", way, 0), ("lower", way, 1)))
    by_way(corner_way, lambda way: all_sent(("first", way, 0), ("first", way, 1)))
    by_way(helper_way, lambda way: all_sent(("second", way), ("third", 1 - way, 0), ("third", 1 - way, 1)))


def step(level_set, image):
    consts = [jnp.asarray(t) for t in tables()]
    ext = pltpu.VMEM((ZE, YE, N), F32)
    half = pltpu.VMEM((4, ZL, YE, N), BF16)
    rows = 4 * G * 32
    return pl.pallas_call(
        kernel,
        out_shape=jax.ShapeDtypeStruct((ZL, YL, N), F32),
        in_specs=[pl.BlockSpec(memory_space=pltpu.HBM)] * 5,
        out_specs=pl.BlockSpec(memory_space=pltpu.VMEM),
        scratch_shapes=[ext] * 5 + [half, half, pltpu.VMEM((2, rows, 256), BF16), pltpu.VMEM((2, rows, 256), BF16),
                                    pltpu.VMEM((rows, N), F32)]
        + [pltpu.VMEM(c.shape, BF16) for c in consts]
        + [pltpu.VMEM((2, 2, PACKED, N), F32)] * 2 + [pltpu.VMEM((2, 2, 2, 40, N), F32), pltpu.VMEM((2, 2, 4, 24, N), F32)]
        + [pltpu.SemaphoreType.DMA((8,)), pltpu.SemaphoreType.DMA((40,)), pltpu.SemaphoreType.DMA((40,))],
        compiler_params=pltpu.CompilerParams(
            collective_id=0, has_side_effects=True, vmem_limit_bytes=48 * 1024 * 1024),
    )(*[pltpu.with_memory_space_constraint(v, pltpu.HBM) for v in (level_set, image, *consts)])


def solution(mesh):
    return jax.shard_map(
        step,
        mesh=mesh,
        in_specs=(P("col", "row", None), P("col", "row", None)),
        out_specs=P("col", "row", None),
        check_vma=False,
    )
```

```python
import functools
import typing

import jax
import jax.numpy as jnp
import ml_dtypes
import numpy as np
from jax import lax
from jax.experimental import pallas as pl
from jax.experimental.pallas import tpu as pltpu
from jax.sharding import PartitionSpec as P

R = 6
N = 384
ZL, YL = 24, 48
ZE, YE = ZL + 2 * R, YL + 16
EPS = 0.05
SIGMA = 8.0
DT, NU = 0.5, 0.1
G = 4
F32, BF16 = jnp.float32, jnp.bfloat16
MESH = pl.DeviceIdType.MESH

ATAN = (
    0.3183096647262573, -0.10609224438667297, 0.06349188834428787, -0.044272541999816895,
    0.03069206140935421, -0.0177974384278059, 0.006959190126508474, -0.0012906072661280632,
)


class Part(typing.NamedTuple):
    plane: int
    planes: int
    start: int
    size: int


PARTS = {"low": Part(0, R, 0, 40), "high": Part(ZL - R, R, 40, 40), "middle": Part(R, ZL - 2 * R, 80, 72)}
PACKED = 152
WINDOWS = (-32, 160)


def taps():
    offsets = np.arange(-R, R + 1, dtype=np.float64)
    weights = np.exp(-offsets * offsets / (2.0 * SIGMA * SIGMA))
    return weights / weights.sum()


def split(table):
    high = table.astype(np.float32).astype(ml_dtypes.bfloat16)
    low = (table - high.astype(np.float64)).astype(np.float32).astype(ml_dtypes.bfloat16)
    return high, low


def tables():
    weights = taps()

    def tap(distance):
        return weights[R + distance] if abs(distance) <= R else 0.0

    centre = weights[R]
    source = list(range(YL)) + list(range(-8, 0)) + list(range(YL, YL + 8))

    def block(outs, cols):
        one = np.array([[tap(source[c] - o) * centre for c in cols] for o in outs])
        return np.kron(np.eye(G), one)

    inner = block(range(8, 40), range(YL))
    edge = block(list(range(8)) + list(range(40, 48)), range(YE))
    halves = []
    for start, first, outs in ((WINDOWS[0], 0, range(0, N // 2)), (WINDOWS[1], 128, range(N // 2, N))):
        half = np.zeros((256, 256))
        for o in outs:
            for d in range(-R, R + 1):
                half[o + d - start, o - first] = weights[R + d]
        high, low = split(half)
        halves.append(np.concatenate([high, high, low]))
    return tuple(np.concatenate(split(t)) for t in (inner, edge)) + (np.stack(halves),)


def heaviside(level):
    big = jnp.abs(level) > 1.0
    t = jnp.where(big, 1.0 / jnp.where(big, level, 1.0), level)
    u = t * t
    q = jnp.full_like(u, ATAN[-1])
    for coeff in ATAN[-2::-1]:
        q = q * u + coeff
    q = q * t
    return jnp.where(big, jnp.where(level > 0.0, 1.0, 0.0) - q, 0.5 + q)


def kernel(level_hbm, image_hbm, y_in, y_ed, x_all, out_ref,
           lev, img, hv, hi, ii, g_h, g_l, xs_h, xs_l, sm,
           t_yi, t_ye, t_x,
           packed, halo, corner, relay, local_sem, send_sem, recv_sem):
    row, col = lax.axis_index("row"), lax.axis_index("col")
    n_row, n_col = lax.axis_size("row"), lax.axis_size("col")
    r_up, r_dn = lax.rem(row + 1, n_row), lax.rem(row + n_row - 1, n_row)
    c_up, c_dn = lax.rem(col + 1, n_col), lax.rem(col + n_col - 1, n_col)

    barrier = pltpu.get_barrier_semaphore()
    for device in ({"row": row, "col": c_up}, {"row": row, "col": c_dn}, {"row": r_up, "col": col}, {"row": r_dn, "col": col}):
        pl.semaphore_signal(barrier, inc=1, device_id=device, device_id_type=MESH)

    own = []
    for i, (src, dst) in enumerate((
        (level_hbm, lev.at[R:R + ZL, 0:YL]), (image_hbm, img.at[R:R + ZL, 0:YL]),
        (y_in, t_yi), (y_ed, t_ye), (x_all, t_x),
    )):
        copy = pltpu.make_async_copy(src, dst, local_sem.at[i])
        copy.start()
        own.append(copy)

    for side in (0, 1):
        for a in (0, 1):
            for part in PARTS.values():
                if part.size > 6 * part.planes:
                    packed[side, a, part.start + 6 * part.planes:part.start + part.size, :] = jnp.zeros(
                        (part.size - 6 * part.planes, N), F32)

    def pack(part):
        for side, first in ((0, YL - R), (1, 0)):
            for a, block in enumerate((lev, img)):
                for q in range(part.planes):
                    at = part.start + 6 * q
                    packed[side, a, at:at + 6, :] = block[R + part.plane + q, first:first + 6, :]

    def unpack(src, start, planes, to):
        for side in (0, 1):
            for a, block in enumerate((lev, img)):
                for q in range(planes):
                    at = start + 6 * q
                    row0 = YL + 2 + 6 * side
                    block[to + q, row0:row0 + 6, :] = src[side, a, at:at + 6, :]

    sent, slots = {}, {}

    def send(name, axis, target, src, dst, now=True, lands=None):
        i = len(sent)
        slots[name] = i if lands is None else slots[lands]
        copy = pltpu.make_async_remote_copy(
            src_ref=src, dst_ref=dst, send_sem=send_sem.at[i], recv_sem=recv_sem.at[slots[name]],
            device_id={axis: target}, device_id_type=MESH,
        )
        if now:
            copy.start()
        sent[name] = copy

    def arrived(*names):
        for name in names:
            sent[name].wait_recv()

    def send_part(name):
        part = PARTS[name]
        rows = pl.ds(part.start, part.size)
        for side, target in ((0, r_up), (1, r_dn)):
            send((name, side), "row", target, packed.at[side, :, rows], halo.at[side, :, rows])

    other = row + 1 - 2 * lax.rem(row, 2)
    outer_row = jnp.logical_or(lax.rem(row, 4) == 0, lax.rem(row, 4) == 3)
    wraps = (lax.rem(col, 8) == 7, lax.rem(col, 8) == 0)
    corner_way = [jnp.logical_and(outer_row, w) for w in wraps]
    helper_way = [jnp.logical_and(jnp.logical_not(outer_row), w) for w in wraps]
    arrays = ((level_hbm, lev), (image_hbm, img))
    upper, lower = pl.ds(0, 24), pl.ds(24, 24)
    z_ways = ((c_up, ZL - 2, R - 2, ZL - R, 0), (c_dn, 0, R + ZL, 2, R + ZL + 2))
    for way, (target, two, two_to, four, four_to) in enumerate(z_ways):
        for a, (src, dst) in enumerate(arrays):
            send(("two", way, a), "col", target, src.at[pl.ds(two, 2)], dst.at[pl.ds(two_to, 2), pl.ds(0, YL)], False)
            for name, rows in (("upper", upper), ("lower", lower)):
                send((name, way, a), "col", target, src.at[pl.ds(four, 4), rows], dst.at[pl.ds(four_to, 4), rows], False)
            send(("first", way, a), "row", other, src.at[pl.ds(four, 4), lower], relay.at[0, a], False,
                 ("first", 0, a) if way else None)
        send(("second", way), "col", target, relay.at[0], relay.at[1], False, ("second", 0) if way else None)
    for way, (_, _, _, _, four_to) in enumerate(z_ways):
        for a, (_, dst) in enumerate(arrays):
            send(("third", way, a), "row", other, relay.at[1, a], dst.at[pl.ds(four_to, 4), lower], False,
                 ("lower", way, a))

    def start(*names):
        for name in names:
            sent[name].start()

    def by_way(predicates, action):
        for way in (0, 1):
            pl.when(predicates[way])(functools.partial(action, way))

    def fields(first, count, start, size, step):
        @pl.loop(0, count // 2)
        def _(i):
            planes = pl.ds(first + 2 * i, 2)
            for s in range(start, start + size, step):
                rows = slice(s, s + step)
                h = heaviside(lev[planes, rows, :])
                im = img[planes, rows, :]
                hv[planes, rows, :] = h
                hi[planes, rows, :] = h * im
                ii[planes, rows, :] = im * im

    own[0].wait()
    own[1].wait()
    pack(PARTS["low"])
    pack(PARTS["high"])

    early = jnp.logical_or(lax.rem(row, 4) == 0, col == 0)

    @pl.when(early)
    def _():
        fields(R, ZL, 0, YL, 16)

    pl.semaphore_wait(barrier, 4)
    by_way(corner_way, lambda way: start(("first", way, 0), ("first", way, 1)))
    send_part("low")
    send_part("high")
    pack(PARTS["middle"])
    send_part("middle")
    start(*[("two", way, a) for way in (0, 1) for a in (0, 1)])
    direct_way = [jnp.logical_not(p) for p in corner_way]
    upper_now = [jnp.logical_not(p) for p in helper_way]
    lower_now = [jnp.logical_not(jnp.logical_or(p, q)) for p, q in zip(corner_way, helper_way)]
    by_way(upper_now, lambda way: start(("upper", way, 0), ("upper", way, 1)))
    by_way(lower_now, lambda way: start(("lower", way, 0), ("lower", way, 1)))

    def forward(way):
        arrived(("first", 0, 0), ("first", 0, 1))
        start(("second", way), *[(name, way, a) for name in ("upper", "lower") for a in (0, 1)])

    def deliver(way):
        arrived(("second", 0))
        start(("third", 1 - way, 0), ("third", 1 - way, 1))

    outer = {"corner above": (c_up, PARTS["high"], 0), "corner below": (c_dn, PARTS["low"], 1)}
    for name, (target, part, way) in outer.items():
        send(name, "col", target, halo.at[:, :, pl.ds(part.start, part.size)], corner.at[way], False)

    weights = taps()
    ratio = [float(np.float32(weights[R + d] / weights[R])) for d in range(R + 1)]

    def smooth_z(g, chunk):
        rows = slice(chunk * 16, chunk * 16 + 16)
        waiting = []

        def store():
            for k, o, lanes, high, low in waiting:
                g_h[k, g * G + o, rows, lanes] = high
                g_l[k, g * G + o, rows, lanes] = low
            waiting.clear()

        for k, ref in enumerate((hi, hv, img, ii)):
            for lt in range(3):
                lanes = slice(lt * 128, lt * 128 + 128)
                f = [ref[g * G + j, rows, lanes] for j in range(G + 2 * R)]
                store()
                for o in range(G):
                    total = f[o + R]
                    for d in range(1, R + 1):
                        total = total + ratio[d] * (f[o + R - d] + f[o + R + d])
                    high = total.astype(BF16)
                    waiting.append((k, o, lanes, high, (total - high.astype(F32)).astype(BF16)))
        store()

    def dot(a, b):
        return jnp.dot(a, b, preferred_element_type=F32)

    def smooth_y(g, table, depth, base):
        planes = pl.ds(g * G, G)
        m = table.shape[0] // 2
        high = [g_h[k, planes, 0:depth, :].reshape(G * depth, N) for k in range(4)]
        low = [g_l[k, planes, 0:depth, :].reshape(G * depth, N) for k in range(4)]
        for k in range(0, 4, 2):
            pair = dot(table[...], jnp.concatenate(high[k:k + 2], axis=1))
            pair = pair[0:m] + pair[m:2 * m] + dot(table[0:m, :], jnp.concatenate(low[k:k + 2], axis=1))
            for f in (0, 1):
                y = pair[:, f * N:(f + 1) * N]
                rows = slice((k + f) * 128 + base, (k + f) * 128 + base + m)
                for w, start in enumerate(WINDOWS):
                    part = pltpu.roll(y, -start % N, 1)[:, 0:256]
                    ph = part.astype(BF16)
                    xs_h[w, rows, :] = ph
                    xs_l[w, rows, :] = (part - ph.astype(F32)).astype(BF16)

    def smooth_x():
        for w in (0, 1):
            a = xs_h[w]
            part = dot(jnp.concatenate([a, xs_l[w], a], axis=1), t_x[w])
            if w == 0:
                sm[:, 0:256] = part
            else:
                sm[:, 128:256] = sm[:, 128:256] + part[:, 0:128]
                sm[:, 256:384] = part[:, 128:256]

    def pointwise(p, rows, base, up, down):
        s1, s2, s3, s4 = (sm[base + k * 128:base + k * 128 + 8, :] for k in range(4))
        level = lev[p + R, rows, :]
        im = img[p + R, rows, :]
        inner = s2 + EPS
        outer = 1.0 - s2 + EPS
        rest = s3 - s1
        both = inner * outer
        x1, x2 = s1 * outer, rest * inner
        spread = s4 - s3 * s3 + EPS
        force = (x1 - x2) * (2.0 * im * both - (x1 + x2)) / (both * both * spread * (np.pi * (1.0 + level * level)))
        lap = (lev[p + R + 1, rows, :] + lev[p + R - 1, rows, :] + up + down
               + pltpu.roll(level, 1, 1) + pltpu.roll(level, N - 1, 1) - 6.0 * level)
        return level + DT * (NU * lap + force)

    def inner_points(g):
        for o in range(G):
            p = g * G + o
            for s in range(8, 40, 16):
                done = [pointwise(p, slice(t, t + 8), o * 32 + t - 8, lev[p + R, t + 1:t + 9, :], lev[p + R, t - 1:t + 7, :])
                        for t in (s, s + 8)]
                for t, value in zip((s, s + 8), done):
                    out_ref[p, t:t + 8, :] = value

    sub = lax.broadcasted_iota(jnp.int32, (8, N), 0)

    def edge_points(e):
        for o in range(2 * G):
            p = e * 2 * G + o
            down = jnp.where(sub == 0, pltpu.roll(lev[p + R, YL:YL + 8, :], 1, 0), pltpu.roll(lev[p + R, 0:8, :], 1, 0))
            up = jnp.where(sub == 7, pltpu.roll(lev[p + R, YL + 8:YL + 16, :], 7, 0),
                           pltpu.roll(lev[p + R, 40:48, :], 7, 0))
            first = pointwise(p, slice(0, 8), o * 16, lev[p + R, 1:9, :], down)
            last = pointwise(p, slice(40, 48), o * 16 + 8, up, lev[p + R, 39:47, :])
            out_ref[p, 0:8, :] = first
            out_ref[p, 40:48, :] = last

    def inner(g):
        for chunk in range(3):
            smooth_z(g, chunk)
        smooth_y(g, t_yi, YL, 0)
        smooth_x()
        inner_points(g)

    def edge(e):
        for half in range(2):
            smooth_z(2 * e + half, 3)
            smooth_y(2 * e + half, t_ye, YE, half * 64)
        smooth_x()
        edge_points(e)

    even = lax.rem(col, 2) == 0
    near = jnp.where(even, 1, 0)
    far = 1 - near

    def z_arrived(side, *names):
        by_way((side == 0, side == 1), lambda way: arrived(*[(name, way, a) for name in names for a in (0, 1)]))

    def corner_halo(side):
        for way, name in ((0, "corner above"), (1, "corner below")):
            @pl.when(side == way)
            def _():
                arrived(name)
                unpack(corner.at[way], 0, R, way * (R + ZL))
        fields(side * (R + ZL), R, YL, 16, 16)

    for block in (lev, img):
        block[:, YL:YE, :] = jnp.zeros((ZE, YE - YL, N), F32)
    @pl.when(jnp.logical_not(early))
    def _():
        fields(R, ZL, 0, YL, 16)

    for copy in own[2:]:
        copy.wait()

    @pl.loop(0, 4)
    def _(i):
        @pl.when(i == 1)
        def _():
            by_way(helper_way, forward)

        @pl.when(i == 2)
        def _():
            z_arrived(near, "two", "upper", "lower")
            fields(near * (R + ZL), R, 0, YL, 16)

        inner(jnp.where(i < 2, i + 2, near * 4 + i - 2))

    by_way(helper_way, deliver)

    arrived(("low", 0), ("low", 1), ("high", 0), ("high", 1))
    for name in outer:
        sent[name].start()
    arrived(("middle", 0), ("middle", 1))
    for part in PARTS.values():
        unpack(halo, part.start, part.planes, R + part.plane)
    fields(R, ZL, YL, 16, 16)

    @pl.loop(0, 2)
    def _(i):
        @pl.when(i == 1)
        def _():
            corner_halo(near)

        edge(jnp.where(i == 0, 1, near * 2))

    @pl.loop(0, 2)
    def _(i):
        @pl.when(i == 0)
        def _():
            z_arrived(far, "two")
            fields(far * (R + ZL - 4) + 4, 2, 0, YL, 16)

        @pl.when(i == 1)
        def _():
            z_arrived(far, "upper", "lower")
            fields(far * (R + ZL + 2), 4, 0, YL, 16)

        inner(jnp.where(i == 0, 1 + 3 * far, 5 * far))

    corner_halo(far)
    edge(far * 2)

    def all_sent(*names):
        for name in names:
            sent[name].wait_send()

    held = ("lower", "first", "second", "third")
    all_sent(*[name for name in sent if name[0] not in held])
    by_way(direct_way, lambda way: all_sent(("lower", way, 0), ("lower", way, 1)))
    by_way(corner_way, lambda way: all_sent(("first", way, 0), ("first", way, 1)))
    by_way(helper_way, lambda way: all_sent(("second", way), ("third", 1 - way, 0), ("third", 1 - way, 1)))


def step(level_set, image):
    consts = [jnp.asarray(t) for t in tables()]
    ext = pltpu.VMEM((ZE, YE, N), F32)
    half = pltpu.VMEM((4, ZL, YE, N), BF16)
    rows = 4 * G * 32
    return pl.pallas_call(
        kernel,
        out_shape=jax.ShapeDtypeStruct((ZL, YL, N), F32),
        in_specs=[pl.BlockSpec(memory_space=pltpu.HBM)] * 5,
        out_specs=pl.BlockSpec(memory_space=pltpu.VMEM),
        scratch_shapes=[ext] * 5 + [half, half, pltpu.VMEM((2, rows, 256), BF16), pltpu.VMEM((2, rows, 256), BF16),
                                    pltpu.VMEM((rows, N), F32)]
        + [pltpu.VMEM(c.shape, BF16) for c in consts]
        + [pltpu.VMEM((2, 2, PACKED, N), F32)] * 2 + [pltpu.VMEM((2, 2, 2, 40, N), F32), pltpu.VMEM((2, 2, 4, 24, N), F32)]
        + [pltpu.SemaphoreType.DMA((8,)), pltpu.SemaphoreType.DMA((40,)), pltpu.SemaphoreType.DMA((40,))],
        compiler_params=pltpu.CompilerParams(
            collective_id=0, has_side_effects=True, vmem_limit_bytes=48 * 1024 * 1024),
    )(*[pltpu.with_memory_space_constraint(v, pltpu.HBM) for v in (level_set, image, *consts)])


def solution(mesh):
    return jax.shard_map(
        step,
        mesh=mesh,
        in_specs=(P("col", "row", None), P("col", "row", None)),
        out_specs=P("col", "row", None),
        check_vma=False,
    )
```
